32 devices in a mesh: groups: 2 (over x), tm: 8 (over z, y), space: 2 (over core).
Axes of the slice: x: 2, y: 2, z: 4, core: 2. Of those that a mesh axis runs over, the one named last changes fastest.
Arguments:
- query_pre: bfloat16 [16, 8, 32, 2240], P(('groups', 'tm'), 'space'), parts along dimension 0, may hold values from -6 to 6
- key_pre: bfloat16 [16, 8, 32, 2240], P(('groups', 'tm'), 'space'), parts along dimension 0, may hold values from -6 to 6
- value_pre: bfloat16 [16, 8, 32, 2240], P(('groups', 'tm'), 'space'), parts along dimension 0, may hold values from -8 to 8
- grad_out: bfloat16 [16, 8, 32, 2240], P(('groups', 'tm'), 'space'), parts along dimension 0, may hold values from -96 to 96
- conv_taps: float32 [3, 3, 2240], replicated, may hold values from -4 to 4
Outputs:
- attended: bfloat16 [16, 8, 32, 2240], P(('groups', 'tm'), 'space'), parts along dimension 0
- query_grad: bfloat16 [16, 8, 32, 2240], P(('groups', 'tm'), 'space'), parts along dimension 0
- key_grad: bfloat16 [16, 8, 32, 2240], P(('groups', 'tm'), 'space'), parts along dimension 0
- value_grad: bfloat16 [16, 8, 32, 2240], P(('groups', 'tm'), 'space'), parts along dimension 0
- taps_grad: float32 [6, 3, 2240], P('groups'), parts along dimension 0
The draws below stay inside these ranges and needn't reach their ends.
There are 2 independent parts, one for each index of `groups`. The reference program is written for one: setup_inputs(seed, part) draws one part's arguments, and reference() takes and returns one part's arrays. A program takes and returns all parts, laid end to end along the dimension named above; an argument that names none is the same for every part. Nothing has to cross between parts.
All inputs are finite; a program needn't handle non-finite values.
Results may differ from the reference program's by a relative error of at most 0.013.
Values may be sent and summed in bfloat16 or wider, within the bound.
A program may use at most 128 MiB of HBM per device.

```python
import jax
import jax.numpy as jnp
from jax import lax

HEADS = 20
HEAD_DIM = 112
COLS = 32
D = 2240
FRAMES = 8
ROWS = 8


def draw_value_pre(key, part):
    first, second, third = jax.random.split(jax.random.fold_in(key, 71), 3)
    frame_mean = jax.random.normal(first, (FRAMES, 1, 1, D), jnp.float32)
    row_mean = 0.5 * jax.random.normal(second, (FRAMES, ROWS, 1, D), jnp.float32)
    noise = jax.random.normal(third, (FRAMES, ROWS, COLS, D), jnp.float32)
    drawn = frame_mean + row_mean + noise
    return jnp.clip(drawn, -8.0, 8.0).astype(jnp.bfloat16)


def level_of(rng, extent, cuts, low, high):
    gain, own = 1.0, jax.random.fold_in(rng, 6)
    for position, blocks in cuts:
        draws = jnp.exp(jax.random.uniform(jax.random.fold_in(own, position), (blocks,), jnp.float32, low / len(cuts), high / len(cuts)))
        gain = gain * jnp.repeat(draws, extent[position] // blocks).reshape([-1 if axis == position else 1 for axis in range(len(extent))])
    return gain


def bell_draw(key, dims, width, most, pieces=(), dtype=jnp.bfloat16):
    values = jax.random.normal(key, dims, jnp.float32) * width
    if len(pieces) > 0:
        values = level_of(key, dims, pieces, -0.22, 0.18) * values
    return jnp.clip(values, min=-most, max=most).astype(dtype)


def setup_inputs(seed: int = 0, part: int = 0) -> dict:
    splits = jax.random.split(jax.random.key(seed), 6)
    part_keys = jax.random.split(jax.random.fold_in(splits[5], part), 6)
    return {
        "query_pre": bell_draw(part_keys[0], (FRAMES, ROWS, COLS, D), 1.0, 6.0, ((0, 8), (1, 2))),
        "key_pre": bell_draw(part_keys[1], (FRAMES, ROWS, COLS, D), 1.0, 6.0, ((0, 8), (1, 2))),
        "value_pre": draw_value_pre(jax.random.fold_in(jax.random.fold_in(splits[5], part), 71), part),
        "grad_out": bell_draw(part_keys[3], (FRAMES, ROWS, COLS, D), 16.0, 96.0, ((0, 8), (1, 2))),
        "conv_taps": bell_draw(splits[4], (3, 3, D), 0.25, 4.0, (), jnp.float32),
    }


def mix_rows(padded, conv_taps, row_count, col_count, flipped):
    summed = jnp.zeros(padded.shape[:1] + (row_count, col_count, padded.shape[3]), jnp.float32)
    for row_off in range(3):
        for col_off in range(3):
            if flipped:
                window = padded[:, 2 - row_off:2 - row_off + row_count, 2 - col_off:2 - col_off + col_count]
            else:
                window = padded[:, row_off:row_off + row_count, col_off:col_off + col_count]
            summed = summed + conv_taps[row_off, col_off] * window
    return summed


def reference(query_pre, key_pre, value_pre, grad_out, conv_taps):
    frame_count, row_count, col_count, model_width = value_pre.shape
    head_count = HEADS
    head_size = HEAD_DIM
    split = (frame_count, row_count * col_count, head_count, head_size)
    highest = lax.Precision.HIGHEST
    value_pad = jnp.pad(value_pre.astype(jnp.float32), ((0, 0), (1, 1), (1, 1), (0, 0)))
    local = mix_rows(value_pad, conv_taps, row_count, col_count, False)
    queries = jnp.maximum(query_pre, 0).astype(jnp.float32).reshape(split)
    keys = jnp.maximum(key_pre, 0).astype(jnp.float32).reshape(split)
    values = value_pre.astype(jnp.float32).reshape(split)
    partial_value = jnp.einsum("fthe,fthd->fhed", keys, values, precision=highest)
    key_sum = jnp.sum(keys, axis=1)
    kv_state = jnp.cumsum(partial_value, axis=0)
    key_total = jnp.cumsum(key_sum, axis=0)
    numerator = jnp.einsum("fthe,fhed->fthd", queries, kv_state, precision=highest)
    denominator = jnp.einsum("fthe,fhe->fth", queries, key_total, precision=highest) + 1.0
    output_f32 = numerator / denominator[..., None]
    attended = (output_f32.reshape(value_pre.shape) + local).astype(jnp.bfloat16)
    cotangent = grad_out.astype(jnp.float32).reshape(split)
    grad_num = cotangent / denominator[..., None]
    grad_den = -jnp.sum(cotangent * output_f32, axis=-1) / denominator
    grad_query = jnp.einsum("fthd,fhed->fthe", grad_num, kv_state, precision=highest) + grad_den[..., None] * key_total[:, None]
    grad_partial = jnp.einsum("fthe,fthd->fhed", queries, grad_num, precision=highest)
    grad_keysum = jnp.einsum("fth,fthe->fhe", grad_den, queries, precision=highest)
    grad_state = jnp.flip(jnp.cumsum(jnp.flip(grad_partial, 0), axis=0), 0)
    grad_total = jnp.flip(jnp.cumsum(jnp.flip(grad_keysum, 0), axis=0), 0)
    grad_key = jnp.einsum("fthd,fhed->fthe", values, grad_state, precision=highest) + grad_total[:, None]
    grad_mixed = jnp.einsum("fthe,fhed->fthd", keys, grad_state, precision=highest).reshape(value_pre.shape)
    query_grad = jnp.where(query_pre > 0, grad_query.reshape(value_pre.shape), 0.0).astype(jnp.bfloat16)
    key_grad = jnp.where(key_pre > 0, grad_key.reshape(value_pre.shape), 0.0).astype(jnp.bfloat16)
    grad_pad = jnp.pad(grad_out.astype(jnp.float32), ((0, 0), (1, 1), (1, 1), (0, 0)))
    value_grad = (grad_mixed + mix_rows(grad_pad, conv_taps, row_count, col_count, True)).astype(jnp.bfloat16)
    cotangent_full = grad_out.astype(jnp.float32)
    tap_rows = []
    for row_off in range(3):
        tap_cols = []
        for col_off in range(3):
            window = value_pad[:, row_off:row_off + row_count, col_off:col_off + col_count]
            tap_cols.append(jnp.sum(cotangent_full * window, axis=(0, 1, 2)))
        tap_rows.append(jnp.stack(tap_cols))
    taps_grad = jnp.stack(tap_rows)
    return attended, query_grad, key_grad, value_grad, taps_grad
```

```python
import jax
import jax.numpy as jnp
from jax import lax
from jax.experimental import pallas as pl
from jax.experimental.pallas import tpu as pltpu
from jax.sharding import PartitionSpec as P

HEADS = 20
HEAD_DIM = 112
LANES = 128
F32 = jnp.float32
BF16 = jnp.bfloat16
VMEM_LIMIT = 60 * 1024 * 1024


def call(body, out_shape, *args):
    return pl.pallas_call(
        body,
        out_shape=out_shape,
        in_specs=[pl.BlockSpec(memory_space=pltpu.VMEM)] * len(args),
        out_specs=jax.tree.map(lambda _: pl.BlockSpec(memory_space=pltpu.VMEM), out_shape),
        compiler_params=pltpu.CompilerParams(vmem_limit_bytes=VMEM_LIMIT),
    )(*args)


def struct(shape, dtype):
    return jax.ShapeDtypeStruct(shape, dtype)


def dot(a, b, dims):
    return lax.dot_general(a, b, (dims, ((), ())), preferred_element_type=F32)


def high_low(x):
    high = x.astype(BF16).astype(F32)
    return high, x - high


def conv_body(rows, cols, value_ref, grad_ref, taps_ref, local_ref, conv_ref, taps_grad_ref):
    width = value_ref.shape[1]
    count = rows * cols
    for low in range(0, width, LANES):
        lanes = slice(low, min(low + LANES, width))
        value = value_ref[:, lanes].astype(F32)
        grad = grad_ref[:, lanes].astype(F32)
        col = lax.broadcasted_iota(jnp.int32, value.shape, 0) % cols
        total = value.shape[0]

        def left(x):
            return jnp.where(col == 0, 0.0, pltpu.roll(x, 1, 0))

        def right(x):
            return jnp.where(col == cols - 1, 0.0, pltpu.roll(x, total - 1, 0))

        values = (left(value), value, right(value))
        grads = (right(grad), grad, left(grad))
        centre = grad[cols : cols + count]
        local = conv = None
        for a in range(3):
            for b in range(3):
                tap = taps_ref[3 * a + b : 3 * a + b + 1, lanes]
                window = values[b][a * cols : a * cols + count]
                back = grads[b][(2 - a) * cols : (2 - a) * cols + count]
                local = tap * window if local is None else local + tap * window
                conv = tap * back if conv is None else conv + tap * back
                taps_grad_ref[3 * a + b : 3 * a + b + 1, lanes] = jnp.sum(
                    centre * window, axis=0, keepdims=True
                )
        local_ref[:, lanes] = local
        conv_ref[:, lanes] = conv


def guarded(x):
    return jnp.where(x > 0, 1.0 / jnp.where(x > 0, x, 1.0), 0.0)


def partial_body(key_ref, value_ref, out_ref):
    size = HEAD_DIM
    count = key_ref.shape[0]
    ones = jnp.where(
        lax.broadcasted_iota(jnp.int32, (count, LANES - size), 1) == 0, 1.0, 0.0
    ).astype(BF16)
    lane = lax.broadcasted_iota(jnp.int32, (size, LANES), 1)
    lane_row = lax.broadcasted_iota(jnp.int32, (1, LANES), 1)
    extra = lax.broadcasted_iota(jnp.int32, (LANES - size, LANES), 0)
    pad = jnp.zeros((1, LANES - size), F32)
    for head in range(HEADS):
        lanes = slice(head * size, (head + 1) * size)
        key = jnp.maximum(key_ref[:, lanes], 0)
        value = jnp.concatenate([value_ref[:, lanes], ones], axis=1)
        sums = dot(key, value, ((0,), (0,)))
        keys = sums[:, size : size + 1]
        inverse = guarded(jnp.sum(keys, axis=0, keepdims=True))
        mean = jnp.where(lane_row < size, jnp.sum(sums, axis=0, keepdims=True) * inverse, 0.0)
        keys_row = jnp.concatenate(
            [jnp.sum(key.astype(F32), axis=0, keepdims=True), pad], axis=1
        )
        out_ref[head] = join(sums - keys * mean, keys, keys_row, mean, lane, extra).astype(BF16)


def join(centred, keys, keys_row, mean, lane, extra):
    size = HEAD_DIM
    high, low = high_low(keys)
    top = jnp.where(
        lane < size, centred, jnp.where(lane == size, high, jnp.where(lane == size + 1, low, 0.0))
    )
    mean_high, mean_low = high_low(mean)
    row_high, row_low = high_low(keys_row)
    bottom = jnp.where(
        extra == 0,
        mean_high,
        jnp.where(extra == 1, mean_low, jnp.where(extra == 2, row_high, jnp.where(extra == 3, row_low, 0.0))),
    )
    return jnp.concatenate([top, bottom], axis=0)


def parts_of(packed):
    size = HEAD_DIM
    top = packed[:size]
    keys = top[:, size : size + 1] + top[:, size + 1 : size + 2]
    mean = packed[size : size + 1] + packed[size + 1 : size + 2]
    keys_row = packed[size + 2 : size + 3] + packed[size + 3 : size + 4]
    return top, keys, keys_row, mean


def merge_packed(first, second, lane, extra):
    top_a, keys_a, row_a, mean_a = parts_of(first)
    top_b, keys_b, row_b, mean_b = parts_of(second)
    mass_a = jnp.sum(keys_a, axis=0, keepdims=True)
    mass_b = jnp.sum(keys_b, axis=0, keepdims=True)
    mean = (mass_a * mean_a + mass_b * mean_b) * guarded(mass_a + mass_b)
    centred = top_a + top_b + keys_a * (mean_a - mean) + keys_b * (mean_b - mean)
    return join(centred, keys_a + keys_b, row_a + row_b, mean, lane, extra)


def merge_body(state_ref, other_ref, out_ref, send_ref):
    size = HEAD_DIM
    lane = lax.broadcasted_iota(jnp.int32, (size, LANES), 1)
    extra = lax.broadcasted_iota(jnp.int32, (LANES - size, LANES), 0)
    for head in range(state_ref.shape[0]):
        merged = merge_packed(
            state_ref[head].astype(F32), other_ref[head].astype(F32), lane, extra
        )
        out_ref[head] = merged
        send_ref[head] = merged.astype(BF16)


def add_body(state_ref, other_ref, out_ref, send_ref):
    size = HEAD_DIM
    lane = lax.broadcasted_iota(jnp.int32, (size, LANES), 1)
    for head in range(state_ref.shape[0]):
        merged = state_ref[head].astype(F32) + other_ref[head].astype(F32)
        sums = merged[:, size : size + 1] + merged[:, size + 1 : size + 2]
        high, low = high_low(sums)
        merged = jnp.where(
            lane < size, merged, jnp.where(lane == size, high, jnp.where(lane == size + 1, low, 0.0))
        )
        out_ref[head] = merged
        send_ref[head] = merged.astype(BF16)


def forward_body(query_ref, grad_ref, local_ref, state_ref, attended_ref, query_grad_ref, out_ref):
    size = HEAD_DIM
    count = query_ref.shape[0]
    lane = lax.broadcasted_iota(jnp.int32, (size, LANES), 1)
    tail = lax.broadcasted_iota(jnp.int32, (count, LANES - size), 1)
    for head in range(HEADS):
        lanes = slice(head * size, (head + 1) * size)
        query_pre = query_ref[:, lanes]
        query = jnp.maximum(query_pre, 0)
        grad = grad_ref[:, lanes]
        cotangent = grad.astype(F32)
        state = state_ref[head]
        mixed = dot(query, state[:size], ((1,), (0,)))
        back = dot(grad, state[:, :size], ((1,), (1,)))
        centred = mixed[:, :size]
        mass = mixed[:, size : size + 1] + mixed[:, size + 1 : size + 2]
        inverse = 1.0 / (mass + 1.0)
        rows = state[size:].astype(F32)
        mean = rows[0:1, :size] + rows[1:2, :size]
        keys_row = rows[2:3, :size] + rows[3:4, :size]
        output = (centred + mass * mean) * inverse
        attended_ref[:, lanes] = (output + local_ref[:, lanes]).astype(BF16)
        along = back[:, size : size + 1] + back[:, size + 1 : size + 2]
        product = jnp.sum(cotangent * centred, axis=1, keepdims=True)
        grad_query = (back[:, :size] + ((along - product) * inverse) * keys_row) * inverse
        query_grad_ref[:, lanes] = jnp.where(
            query_pre.astype(F32) > 0, grad_query, 0.0
        ).astype(BF16)
        high, low = high_low(-(product + mass * along) * inverse)
        side = jnp.where(tail == 0, high, jnp.where(tail == 1, low, 0.0)).astype(BF16)
        scaled = (query.astype(F32) * inverse).astype(BF16)
        sums = dot(scaled, jnp.concatenate([grad, side], axis=1), ((0,), (0,)))
        total = sums[:, size : size + 1] + sums[:, size + 1 : size + 2]
        high, low = high_low(total)
        out_ref[head] = jnp.where(
            lane < size, sums, jnp.where(lane == size, high, jnp.where(lane == size + 1, low, 0.0))
        ).astype(BF16)


def backward_body(key_ref, value_ref, conv_ref, state_ref, key_grad_ref, value_grad_ref):
    size = HEAD_DIM
    count = key_ref.shape[0]
    ones = jnp.where(
        lax.broadcasted_iota(jnp.int32, (count, LANES - size), 1) < 2, 1.0, 0.0
    ).astype(BF16)
    for head in range(HEADS):
        lanes = slice(head * size, (head + 1) * size)
        key_pre = key_ref[:, lanes]
        state = state_ref[head]
        value = jnp.concatenate([value_ref[:, lanes], ones], axis=1)
        grad_key = dot(value, state, ((1,), (1,)))
        mixed = dot(jnp.maximum(key_pre, 0), state, ((1,), (0,)))
        key_grad_ref[:, lanes] = jnp.where(key_pre.astype(F32) > 0, grad_key, 0.0).astype(BF16)
        value_grad_ref[:, lanes] = (mixed[:, :size] + conv_ref[:, lanes]).astype(BF16)


def with_edges(block):
    count = lax.axis_size("space")
    forward = [(i, i + 1) for i in range(count - 1)]
    backward = [(i + 1, i) for i in range(count - 1)]
    low = lax.ppermute(block[:, -1:], "space", forward)
    high = lax.ppermute(block[:, :1], "space", backward)
    return jnp.concatenate([low, block, high], axis=1)


def scan_over(local, body, reverse):
    half = local.shape[0] // 2
    place = lax.axis_index("space")
    count = lax.axis_size("tm")
    swap = [(0, 1), (1, 0)]
    own = lax.dynamic_slice_in_dim(local, place * half, half, 0)
    away = lax.dynamic_slice_in_dim(local, (1 - place) * half, half, 0)
    shape = (struct(own.shape, F32), struct(own.shape, BF16))
    state, send = call(body, shape, own, lax.ppermute(away, "space", swap))
    step = 1
    while step < count:
        pairs = [(i, i + step) for i in range(count - step)]
        if reverse:
            pairs = [(b, a) for a, b in pairs]
        state, send = call(body, shape, state, lax.ppermute(send, "tm", pairs))
        step *= 2
    other = lax.ppermute(send, "space", swap)
    return jnp.where(
        place == 0, jnp.concatenate([send, other], 0), jnp.concatenate([other, send], 0)
    )


def shards(query_pre, key_pre, value_pre, grad_out, conv_taps):
    frames, rows, cols, width = value_pre.shape
    assert frames == 1 and width == HEADS * HEAD_DIM and lax.axis_size("space") == 2
    count = rows * cols
    flat = (count, width)
    query, key, value, grad = (
        a.reshape(flat) for a in (query_pre, key_pre, value_pre, grad_out)
    )
    partial = call(partial_body, struct((HEADS, LANES, LANES), BF16), key, value)
    value_rows = with_edges(value_pre).reshape((rows + 2) * cols, width)
    grad_rows = with_edges(grad_out).reshape((rows + 2) * cols, width)
    local, conv, taps_grad = call(
        lambda *refs: conv_body(rows, cols, *refs),
        (struct(flat, F32), struct(flat, F32), struct((9, width), F32)),
        value_rows,
        grad_rows,
        conv_taps.reshape(9, width),
    )
    taps_grad = lax.psum(taps_grad, ("tm", "space")).reshape(3, 3, width)
    state = scan_over(partial, merge_body, False)
    attended, query_grad, grad_partial = call(
        forward_body,
        (struct(flat, BF16), struct(flat, BF16), struct((HEADS, HEAD_DIM, LANES), BF16)),
        query,
        grad,
        local,
        state,
    )
    grad_state = scan_over(grad_partial, add_body, True)
    key_grad, value_grad = call(
        backward_body,
        (struct(flat, BF16), struct(flat, BF16)),
        key,
        value,
        conv,
        grad_state,
    )
    full = value_pre.shape
    return (
        attended.reshape(full),
        query_grad.reshape(full),
        key_grad.reshape(full),
        value_grad.reshape(full),
        taps_grad,
    )


def solution(mesh):
    tokens = P(("groups", "tm"), "space", None, None)
    return jax.shard_map(
        shards,
        mesh=mesh,
        in_specs=(tokens, tokens, tokens, tokens, P()),
        out_specs=(tokens, tokens, tokens, tokens, P("groups", None, None)),
        check_vma=False,
    )
```

```python
import jax
import jax.numpy as jnp
from jax import lax
from jax.experimental import pallas as pl
from jax.experimental.pallas import tpu as pltpu
from jax.sharding import PartitionSpec as P

HEADS = 20
HEAD_DIM = 112
LANES = 128
F32 = jnp.float32
BF16 = jnp.bfloat16
VMEM_LIMIT = 60 * 1024 * 1024


def call(body, out_shape, *args):
    return pl.pallas_call(
        body,
        out_shape=out_shape,
        in_specs=[pl.BlockSpec(memory_space=pltpu.VMEM)] * len(args),
        out_specs=jax.tree.map(lambda _: pl.BlockSpec(memory_space=pltpu.VMEM), out_shape),
        compiler_params=pltpu.CompilerParams(vmem_limit_bytes=VMEM_LIMIT),
    )(*args)


def struct(shape, dtype):
    return jax.ShapeDtypeStruct(shape, dtype)


def dot(a, b, dims):
    return lax.dot_general(a, b, (dims, ((), ())), preferred_element_type=F32)


def high_low(x):
    high = x.astype(BF16).astype(F32)
    return high, x - high


def conv_body(rows, cols, value_ref, grad_ref, taps_ref, local_ref, conv_ref, taps_grad_ref):
    width = value_ref.shape[1]
    count = rows * cols
    for low in range(0, width, LANES):
        lanes = slice(low, min(low + LANES, width))
        value = value_ref[:, lanes].astype(F32)
        grad = grad_ref[:, lanes].astype(F32)
        col = lax.broadcasted_iota(jnp.int32, value.shape, 0) % cols
        total = value.shape[0]

        def left(x):
            return jnp.where(col == 0, 0.0, pltpu.roll(x, 1, 0))

        def right(x):
            return jnp.where(col == cols - 1, 0.0, pltpu.roll(x, total - 1, 0))

        values = (left(value), value, right(value))
        grads = (right(grad), grad, left(grad))
        centre = grad[cols : cols + count]
        local = conv = None
        for a in range(3):
            for b in range(3):
                tap = taps_ref[3 * a + b : 3 * a + b + 1, lanes]
                window = values[b][a * cols : a * cols + count]
                back = grads[b][(2 - a) * cols : (2 - a) * cols + count]
                local = tap * window if local is None else local + tap * window
                conv = tap * back if conv is None else conv + tap * back
                taps_grad_ref[3 * a + b : 3 * a + b + 1, lanes] = jnp.sum(
                    centre * window, axis=0, keepdims=True
                )
        local_ref[:, lanes] = local
        conv_ref[:, lanes] = conv


def guarded(x):
    return jnp.where(x > 0, 1.0 / jnp.where(x > 0, x, 1.0), 0.0)


def partial_body(key_ref, value_ref, out_ref):
    size = HEAD_DIM
    count = key_ref.shape[0]
    ones = jnp.where(
        lax.broadcasted_iota(jnp.int32, (count, LANES - size), 1) == 0, 1.0, 0.0
    ).astype(BF16)
    lane = lax.broadcasted_iota(jnp.int32, (size, LANES), 1)
    lane_row = lax.broadcasted_iota(jnp.int32, (1, LANES), 1)
    extra = lax.broadcasted_iota(jnp.int32, (LANES - size, LANES), 0)
    pad = jnp.zeros((1, LANES - size), F32)
    for head in range(HEADS):
        lanes = slice(head * size, (head + 1) * size)
        key = jnp.maximum(key_ref[:, lanes], 0)
        value = jnp.concatenate([value_ref[:, lanes], ones], axis=1)
        sums = dot(key, value, ((0,), (0,)))
        keys = sums[:, size : size + 1]
        inverse = guarded(jnp.sum(keys, axis=0, keepdims=True))
        mean = jnp.where(lane_row < size, jnp.sum(sums, axis=0, keepdims=True) * inverse, 0.0)
        keys_row = jnp.concatenate(
            [jnp.sum(key.astype(F32), axis=0, keepdims=True), pad], axis=1
        )
        out_ref[head] = join(sums - keys * mean, keys, keys_row, mean, lane, extra).astype(BF16)


def join(centred, keys, keys_row, mean, lane, extra):
    size = HEAD_DIM
    high, low = high_low(keys)
    top = jnp.where(
        lane < size, centred, jnp.where(lane == size, high, jnp.where(lane == size + 1, low, 0.0))
    )
    mean_high, mean_low = high_low(mean)
    row_high, row_low = high_low(keys_row)
    bottom = jnp.where(
        extra == 0,
        mean_high,
        jnp.where(extra == 1, mean_low, jnp.where(extra == 2, row_high, jnp.where(extra == 3, row_low, 0.0))),
    )
    return jnp.concatenate([top, bottom], axis=0)


def parts_of(packed):
    size = HEAD_DIM
    top = packed[:size]
    keys = top[:, size : size + 1] + top[:, size + 1 : size + 2]
    mean = packed[size : size + 1] + packed[size + 1 : size + 2]
    keys_row = packed[size + 2 : size + 3] + packed[size + 3 : size + 4]
    return top, keys, keys_row, mean


def merge_packed(first, second, lane, extra):
    top_a, keys_a, row_a, mean_a = parts_of(first)
    top_b, keys_b, row_b, mean_b = parts_of(second)
    mass_a = jnp.sum(keys_a, axis=0, keepdims=True)
    mass_b = jnp.sum(keys_b, axis=0, keepdims=True)
    mean = (mass_a * mean_a + mass_b * mean_b) * guarded(mass_a + mass_b)
    centred = top_a + top_b + keys_a * (mean_a - mean) + keys_b * (mean_b - mean)
    return join(centred, keys_a + keys_b, row_a + row_b, mean, lane, extra)


def merge_body(state_ref, other_ref, out_ref, send_ref):
    size = HEAD_DIM
    lane = lax.broadcasted_iota(jnp.int32, (size, LANES), 1)
    extra = lax.broadcasted_iota(jnp.int32, (LANES - size, LANES), 0)
    for head in range(state_ref.shape[0]):
        merged = merge_packed(
            state_ref[head].astype(F32), other_ref[head].astype(F32), lane, extra
        )
        out_ref[head] = merged
        send_ref[head] = merged.astype(BF16)


def add_body(state_ref, other_ref, out_ref, send_ref):
    size = HEAD_DIM
    lane = lax.broadcasted_iota(jnp.int32, (size, LANES), 1)
    for head in range(state_ref.shape[0]):
        merged = state_ref[head].astype(F32) + other_ref[head].astype(F32)
        sums = merged[:, size : size + 1] + merged[:, size + 1 : size + 2]
        high, low = high_low(sums)
        merged = jnp.where(
            lane < size, merged, jnp.where(lane == size, high, jnp.where(lane == size + 1, low, 0.0))
        )
        out_ref[head] = merged
        send_ref[head] = merged.astype(BF16)


def forward_body(query_ref, grad_ref, local_ref, state_ref, attended_ref, query_grad_ref, out_ref):
    size = HEAD_DIM
    count = query_ref.shape[0]
    lane = lax.broadcasted_iota(jnp.int32, (size, LANES), 1)
    tail = lax.broadcasted_iota(jnp.int32, (count, LANES - size), 1)
    for head in range(HEADS):
        lanes = slice(head * size, (head + 1) * size)
        query_pre = query_ref[:, lanes]
        query = jnp.maximum(query_pre, 0)
        grad = grad_ref[:, lanes]
        cotangent = grad.astype(F32)
        state = state_ref[head]
        mixed = dot(query, state[:size], ((1,), (0,)))
        back = dot(grad, state[:, :size], ((1,), (1,)))
        centred = mixed[:, :size]
        mass = mixed[:, size : size + 1] + mixed[:, size + 1 : size + 2]
        inverse = 1.0 / (mass + 1.0)
        rows = state[size:].astype(F32)
        mean = rows[0:1, :size] + rows[1:2, :size]
        keys_row = rows[2:3, :size] + rows[3:4, :size]
        output = (centred + mass * mean) * inverse
        attended_ref[:, lanes] = (output + local_ref[:, lanes]).astype(BF16)
        along = back[:, size : size + 1] + back[:, size + 1 : size + 2]
        product = jnp.sum(cotangent * centred, axis=1, keepdims=True)
        grad_query = (back[:, :size] + ((along - product) * inverse) * keys_row) * inverse
        query_grad_ref[:, lanes] = jnp.where(
            query_pre.astype(F32) > 0, grad_query, 0.0
        ).astype(BF16)
        high, low = high_low(-(product + mass * along) * inverse)
        side = jnp.where(tail == 0, high, jnp.where(tail == 1, low, 0.0)).astype(BF16)
        scaled = (query.astype(F32) * inverse).astype(BF16)
        sums = dot(scaled, jnp.concatenate([grad, side], axis=1), ((0,), (0,)))
        total = sums[:, size : size + 1] + sums[:, size + 1 : size + 2]
        high, low = high_low(total)
        out_ref[head] = jnp.where(
            lane < size, sums, jnp.where(lane == size, high, jnp.where(lane == size + 1, low, 0.0))
        ).astype(BF16)


def backward_body(key_ref, value_ref, conv_ref, state_ref, key_grad_ref, value_grad_ref):
    size = HEAD_DIM
    count = key_ref.shape[0]
    ones = jnp.where(
        lax.broadcasted_iota(jnp.int32, (count, LANES - size), 1) < 2, 1.0, 0.0
    ).astype(BF16)
    for head in range(HEADS):
        lanes = slice(head * size, (head + 1) * size)
        key_pre = key_ref[:, lanes]
        state = state_ref[head]
        value = jnp.concatenate([value_ref[:, lanes], ones], axis=1)
        grad_key = dot(value, state, ((1,), (1,)))
        mixed = dot(jnp.maximum(key_pre, 0), state, ((1,), (0,)))
        key_grad_ref[:, lanes] = jnp.where(key_pre.astype(F32) > 0, grad_key, 0.0).astype(BF16)
        value_grad_ref[:, lanes] = (mixed[:, :size] + conv_ref[:, lanes]).astype(BF16)


def with_edges(block):
    count = lax.axis_size("space")
    forward = [(i, i + 1) for i in range(count - 1)]
    backward = [(i + 1, i) for i in range(count - 1)]
    low = lax.ppermute(block[:, -1:], "space", forward)
    high = lax.ppermute(block[:, :1], "space", backward)
    return jnp.concatenate([low, block, high], axis=1)


def scan_over(local, body, reverse):
    half = local.shape[0] // 2
    place = lax.axis_index("space")
    count = lax.axis_size("tm")
    swap = [(0, 1), (1, 0)]
    own = lax.dynamic_slice_in_dim(local, place * half, half, 0)
    away = lax.dynamic_slice_in_dim(local, (1 - place) * half, half, 0)
    shape = (struct(own.shape, F32), struct(own.shape, BF16))
    state, send = call(body, shape, own, lax.ppermute(away, "space", swap))
    step = 1
    while step < count:
        pairs = [(i, i + step) for i in range(count - step)]
        if reverse:
            pairs = [(b, a) for a, b in pairs]
        state, send = call(body, shape, state, lax.ppermute(send, "tm", pairs))
        step *= 2
    other = lax.ppermute(send, "space", swap)
    return jnp.where(
        place == 0, jnp.concatenate([send, other], 0), jnp.concatenate([other, send], 0)
    )


def summed_over(x, axis):
    count = lax.axis_size(axis)
    if count & (count - 1):
        return lax.psum(x, axis)
    step = 1
    while step < count:
        x = x + lax.ppermute(x, axis, [(i, i ^ step) for i in range(count)])
        step *= 2
    return x


def shards(query_pre, key_pre, value_pre, grad_out, conv_taps):
    frames, rows, cols, width = value_pre.shape
    assert frames == 1 and width == HEADS * HEAD_DIM and lax.axis_size("space") == 2
    count = rows * cols
    flat = (count, width)
    query, key, value, grad = (
        a.reshape(flat) for a in (query_pre, key_pre, value_pre, grad_out)
    )
    partial = call(partial_body, struct((HEADS, LANES, LANES), BF16), key, value)
    value_rows = with_edges(value_pre).reshape((rows + 2) * cols, width)
    grad_rows = with_edges(grad_out).reshape((rows + 2) * cols, width)
    local, conv, taps_grad = call(
        lambda *refs: conv_body(rows, cols, *refs),
        (struct(flat, F32), struct(flat, F32), struct((9, width), F32)),
        value_rows,
        grad_rows,
        conv_taps.reshape(9, width),
    )
    for axis in ("space", "tm"):
        taps_grad = summed_over(taps_grad, axis)
    taps_grad = taps_grad.reshape(3, 3, width)
    state = scan_over(partial, merge_body, False)
    attended, query_grad, grad_partial = call(
        forward_body,
        (struct(flat, BF16), struct(flat, BF16), struct((HEADS, HEAD_DIM, LANES), BF16)),
        query,
        grad,
        local,
        state,
    )
    grad_state = scan_over(grad_partial, add_body, True)
    key_grad, value_grad = call(
        backward_body,
        (struct(flat, BF16), struct(flat, BF16)),
        key,
        value,
        conv,
        grad_state,
    )
    full = value_pre.shape
    return (
        attended.reshape(full),
        query_grad.reshape(full),
        key_grad.reshape(full),
        value_grad.reshape(full),
        taps_grad,
    )


def solution(mesh):
    tokens = P(("groups", "tm"), "space", None, None)
    return jax.shard_map(
        shards,
        mesh=mesh,
        in_specs=(tokens, tokens, tokens, tokens, P()),
        out_specs=(tokens, tokens, tokens, tokens, P("groups", None, None)),
        check_vma=False,
    )
```

```python
import functools

import jax
import jax.numpy as jnp
from jax import lax
from jax.experimental import pallas as pl
from jax.experimental.pallas import tpu as pltpu
from jax.sharding import PartitionSpec as P

HEADS = 20
HEAD_DIM = 112
LANES = 128
F32 = jnp.float32
BF16 = jnp.bfloat16
VMEM_LIMIT = 60 * 1024 * 1024


def cost(microseconds):
    return pl.CostEstimate(
        flops=int(microseconds * 1e9), bytes_accessed=int(microseconds * 3e6), transcendentals=0
    )


def call(body, out_shape, *args):
    return pl.pallas_call(
        body,
        out_shape=out_shape,
        in_specs=[pl.BlockSpec(memory_space=pltpu.VMEM)] * len(args),
        out_specs=jax.tree.map(lambda _: pl.BlockSpec(memory_space=pltpu.VMEM), out_shape),
        compiler_params=pltpu.CompilerParams(vmem_limit_bytes=VMEM_LIMIT),
        cost_estimate=cost(6),
    )(*args)


def struct(shape, dtype):
    return jax.ShapeDtypeStruct(shape, dtype)


def dot(a, b, dims):
    return lax.dot_general(a, b, (dims, ((), ())), preferred_element_type=F32)


def high_low(x):
    high = x.astype(BF16).astype(F32)
    return high, x - high


def conv_body(rows, cols, value_ref, grad_ref, taps_ref, local_ref, conv_ref, taps_grad_ref):
    width = value_ref.shape[1]
    count = rows * cols
    for low in range(0, width, LANES):
        lanes = slice(low, min(low + LANES, width))
        value = value_ref[:, lanes].astype(F32)
        grad = grad_ref[:, lanes].astype(F32)
        col = lax.broadcasted_iota(jnp.int32, value.shape, 0) % cols
        total = value.shape[0]

        def left(x):
            return jnp.where(col == 0, 0.0, pltpu.roll(x, 1, 0))

        def right(x):
            return jnp.where(col == cols - 1, 0.0, pltpu.roll(x, total - 1, 0))

        values = (left(value), value, right(value))
        grads = (right(grad), grad, left(grad))
        centre = grad[cols : cols + count]
        local = conv = None
        for a in range(3):
            for b in range(3):
                tap = taps_ref[3 * a + b : 3 * a + b + 1, lanes]
                window = values[b][a * cols : a * cols + count]
                back = grads[b][(2 - a) * cols : (2 - a) * cols + count]
                local = tap * window if local is None else local + tap * window
                conv = tap * back if conv is None else conv + tap * back
                taps_grad_ref[3 * a + b : 3 * a + b + 1, lanes] = jnp.sum(
                    centre * window, axis=0, keepdims=True
                )
        local_ref[:, lanes] = local
        conv_ref[:, lanes] = conv


def guarded(x):
    return jnp.where(x > 0, 1.0 / jnp.where(x > 0, x, 1.0), 0.0)


def partial_body(key_ref, value_ref, out_ref):
    size = HEAD_DIM
    count = key_ref.shape[0]
    ones = jnp.where(
        lax.broadcasted_iota(jnp.int32, (count, LANES - size), 1) == 0, 1.0, 0.0
    ).astype(BF16)
    lane = lax.broadcasted_iota(jnp.int32, (size, LANES), 1)
    lane_row = lax.broadcasted_iota(jnp.int32, (1, LANES), 1)
    extra = lax.broadcasted_iota(jnp.int32, (LANES - size, LANES), 0)
    pad = jnp.zeros((1, LANES - size), F32)
    for head in range(HEADS):
        lanes = slice(head * size, (head + 1) * size)
        key = jnp.maximum(key_ref[:, lanes], 0)
        value = jnp.concatenate([value_ref[:, lanes], ones], axis=1)
        sums = dot(key, value, ((0,), (0,)))
        keys = sums[:, size : size + 1]
        inverse = guarded(jnp.sum(keys, axis=0, keepdims=True))
        mean = jnp.where(lane_row < size, jnp.sum(sums, axis=0, keepdims=True) * inverse, 0.0)
        keys_row = jnp.concatenate(
            [jnp.sum(key.astype(F32), axis=0, keepdims=True), pad], axis=1
        )
        out_ref[head] = join(sums - keys * mean, keys, keys_row, mean, lane, extra).astype(BF16)


def join(centred, keys, keys_row, mean, lane, extra):
    size = HEAD_DIM
    high, low = high_low(keys)
    top = jnp.where(
        lane < size, centred, jnp.where(lane == size, high, jnp.where(lane == size + 1, low, 0.0))
    )
    mean_high, mean_low = high_low(mean)
    row_high, row_low = high_low(keys_row)
    bottom = jnp.where(
        extra == 0,
        mean_high,
        jnp.where(extra == 1, mean_low, jnp.where(extra == 2, row_high, jnp.where(extra == 3, row_low, 0.0))),
    )
    return jnp.concatenate([top, bottom], axis=0)


def parts_of(packed):
    size = HEAD_DIM
    top = packed[:size]
    keys = top[:, size : size + 1] + top[:, size + 1 : size + 2]
    mean = packed[size : size + 1] + packed[size + 1 : size + 2]
    keys_row = packed[size + 2 : size + 3] + packed[size + 3 : size + 4]
    return top, keys, keys_row, mean


def merge_packed(first, second, lane, extra):
    top_a, keys_a, row_a, mean_a = parts_of(first)
    top_b, keys_b, row_b, mean_b = parts_of(second)
    mass_a = jnp.sum(keys_a, axis=0, keepdims=True)
    mass_b = jnp.sum(keys_b, axis=0, keepdims=True)
    mean = (mass_a * mean_a + mass_b * mean_b) * guarded(mass_a + mass_b)
    centred = top_a + top_b + keys_a * (mean_a - mean) + keys_b * (mean_b - mean)
    return join(centred, keys_a + keys_b, row_a + row_b, mean, lane, extra)


def add_packed(first, second, lane, extra):
    size = HEAD_DIM
    merged = first + second
    sums = merged[:, size : size + 1] + merged[:, size + 1 : size + 2]
    high, low = high_low(sums)
    return jnp.where(
        lane < size, merged, jnp.where(lane == size, high, jnp.where(lane == size + 1, low, 0.0))
    )


def scan_body(
    merge,
    reverse,
    local_ref,
    out_ref,
    half_ref,
    core_recv,
    pair_send,
    pair_recv,
    chain_send,
    chain_recv,
    core_sems,
    pair_sems,
    chain_sems,
    out_sems,
):
    heads = core_recv.shape[0]
    core = lax.axis_index("space")
    place = lax.axis_index("tm")
    links = lax.axis_size("tm") // 2
    link, side = place // 2, place % 2
    pair = link * 2 + (1 - side)
    if reverse:
        order, ahead, behind, sums_both = links - 1 - link, place - 2, place + 2, side == 0
    else:
        order, ahead, behind, sums_both = link, place + 2, place - 2, side == 1
    lane = lax.broadcasted_iota(jnp.int32, (HEAD_DIM, LANES), 1)
    extra = lax.broadcasted_iota(jnp.int32, (LANES - HEAD_DIM, LANES), 0)

    def remote(source, target, sems, head, device):
        return pltpu.make_async_remote_copy(
            src_ref=source,
            dst_ref=target,
            send_sem=sems.at[0, head],
            recv_sem=sems.at[1, head],
            device_id=device,
            device_id_type=pl.DeviceIdType.MESH,
        )

    def core_copy(head):
        return remote(
            local_ref.at[(1 - core) * heads + head],
            core_recv.at[head],
            core_sems,
            head,
            {"space": 1 - core},
        )

    def pair_copy(head):
        return remote(pair_send.at[head], pair_recv.at[head], pair_sems, head, {"tm": pair})

    def chain_copy(head):
        return remote(chain_send.at[head], chain_recv.at[head], chain_sems, head, {"tm": ahead})

    def out_copy(head):
        mine = out_ref.at[core * heads + head]
        return remote(mine, mine, out_sems, head, {"space": 1 - core})

    barrier = pltpu.get_barrier_semaphore()

    def greet(device):
        pl.semaphore_signal(barrier, inc=1, device_id=device, device_id_type=pl.DeviceIdType.MESH)

    greet({"space": 1 - core})
    greet({"tm": pair})

    @pl.when(order < links - 1)
    def _():
        greet({"tm": ahead})

    @pl.when(order > 0)
    def _():
        greet({"tm": behind})

    @pl.when(order == 0)
    def _():
        chain_recv[...] = jnp.zeros_like(chain_recv)

    peers = 2 + jnp.minimum(order, 1) + jnp.minimum(links - 1 - order, 1)
    pl.semaphore_wait(barrier, peers)

    def begin(head, _):
        core_copy(head).start()
        return 0

    lax.fori_loop(0, heads, begin, 0)

    def over_cores(head, _):
        core_copy(head).wait_recv()
        half = merge(
            local_ref[core * heads + head].astype(F32), core_recv[head].astype(F32), lane, extra
        )
        half_ref[head] = half
        pair_send[head] = half.astype(BF16)
        pair_copy(head).start()
        return 0

    lax.fori_loop(0, heads, over_cores, 0)

    def over_pairs(head, _):
        pair_copy(head).wait_recv()
        half = half_ref[head]
        both = merge(half, pair_recv[head].astype(F32), lane, extra)

        @pl.when(order > 0)
        def _():
            chain_copy(head).wait_recv()

        before = chain_recv[head].astype(F32)

        @pl.when(order < links - 1)
        def _():
            chain_send[head] = merge(before, both, lane, extra).astype(BF16)
            chain_copy(head).start()

        mine = jnp.where(sums_both, both, half)
        out_ref[core * heads + head] = merge(before, mine, lane, extra).astype(BF16)
        out_copy(head).start()
        return 0

    lax.fori_loop(0, heads, over_pairs, 0)

    def finish(head, _):
        core_copy(head).wait_send()
        pair_copy(head).wait_send()

        @pl.when(order < links - 1)
        def _():
            chain_copy(head).wait_send()

        out_copy(head).wait()
        return 0

    lax.fori_loop(0, heads, finish, 0)


def forward_body(query_ref, grad_ref, local_ref, state_ref, attended_ref, query_grad_ref, out_ref):
    size = HEAD_DIM
    count = query_ref.shape[0]
    lane = lax.broadcasted_iota(jnp.int32, (size, LANES), 1)
    tail = lax.broadcasted_iota(jnp.int32, (count, LANES - size), 1)
    for head in range(HEADS):
        lanes = slice(head * size, (head + 1) * size)
        query_pre = query_ref[:, lanes]
        query = jnp.maximum(query_pre, 0)
        grad = grad_ref[:, lanes]
        cotangent = grad.astype(F32)
        state = state_ref[head]
        mixed = dot(query, state[:size], ((1,), (0,)))
        back = dot(grad, state[:, :size], ((1,), (1,)))
        centred = mixed[:, :size]
        mass = mixed[:, size : size + 1] + mixed[:, size + 1 : size + 2]
        inverse = 1.0 / (mass + 1.0)
        rows = state[size:].astype(F32)
        mean = rows[0:1, :size] + rows[1:2, :size]
        keys_row = rows[2:3, :size] + rows[3:4, :size]
        output = (centred + mass * mean) * inverse
        attended_ref[:, lanes] = (output + local_ref[:, lanes]).astype(BF16)
        along = back[:, size : size + 1] + back[:, size + 1 : size + 2]
        product = jnp.sum(cotangent * centred, axis=1, keepdims=True)
        grad_query = (back[:, :size] + ((along - product) * inverse) * keys_row) * inverse
        query_grad_ref[:, lanes] = jnp.where(
            query_pre.astype(F32) > 0, grad_query, 0.0
        ).astype(BF16)
        high, low = high_low(-(product + mass * along) * inverse)
        side = jnp.where(tail == 0, high, jnp.where(tail == 1, low, 0.0)).astype(BF16)
        scaled = (query.astype(F32) * inverse).astype(BF16)
        sums = dot(scaled, jnp.concatenate([grad, side], axis=1), ((0,), (0,)))
        total = sums[:, size : size + 1] + sums[:, size + 1 : size + 2]
        high, low = high_low(total)
        out_ref[head] = jnp.where(
            lane < size, sums, jnp.where(lane == size, high, jnp.where(lane == size + 1, low, 0.0))
        ).astype(BF16)


def backward_body(key_ref, value_ref, conv_ref, state_ref, key_grad_ref, value_grad_ref):
    size = HEAD_DIM
    count = key_ref.shape[0]
    ones = jnp.where(
        lax.broadcasted_iota(jnp.int32, (count, LANES - size), 1) < 2, 1.0, 0.0
    ).astype(BF16)
    for head in range(HEADS):
        lanes = slice(head * size, (head + 1) * size)
        key_pre = key_ref[:, lanes]
        state = state_ref[head]
        value = jnp.concatenate([value_ref[:, lanes], ones], axis=1)
        grad_key = dot(value, state, ((1,), (1,)))
        mixed = dot(jnp.maximum(key_pre, 0), state, ((1,), (0,)))
        key_grad_ref[:, lanes] = jnp.where(key_pre.astype(F32) > 0, grad_key, 0.0).astype(BF16)
        value_grad_ref[:, lanes] = (mixed[:, :size] + conv_ref[:, lanes]).astype(BF16)


def with_edges(block):
    count = lax.axis_size("space")
    forward = [(i, i + 1) for i in range(count - 1)]
    backward = [(i + 1, i) for i in range(count - 1)]
    low = lax.ppermute(block[:, -1:], "space", forward)
    high = lax.ppermute(block[:, :1], "space", backward)
    return jnp.concatenate([low, block, high], axis=1)


def scan_over(local, merge, reverse):
    half = (local.shape[0] // 2,) + local.shape[1:]
    sems = pltpu.SemaphoreType.DMA((2, half[0]))
    return pl.pallas_call(
        functools.partial(scan_body, merge, reverse),
        out_shape=struct(local.shape, BF16),
        in_specs=[pl.BlockSpec(memory_space=pltpu.VMEM)],
        out_specs=pl.BlockSpec(memory_space=pltpu.VMEM),
        scratch_shapes=[pltpu.VMEM(half, F32)] + [pltpu.VMEM(half, BF16)] * 5 + [sems] * 4,
        compiler_params=pltpu.CompilerParams(
            collective_id=int(reverse), has_side_effects=True, vmem_limit_bytes=VMEM_LIMIT
        ),
        cost_estimate=cost(25),
    )(local)


def summed_over(x, axis):
    count = lax.axis_size(axis)
    if count & (count - 1):
        return lax.psum(x, axis)
    step = 1
    while step < count:
        x = x + lax.ppermute(x, axis, [(i, i ^ step) for i in range(count)])
        step *= 2
    return x


def shards(query_pre, key_pre, value_pre, grad_out, conv_taps):
    frames, rows, cols, width = value_pre.shape
    assert frames == 1 and width == HEADS * HEAD_DIM and lax.axis_size("space") == 2
    assert lax.axis_size("tm") % 2 == 0
    count = rows * cols
    flat = (count, width)
    query, key, value, grad = (
        a.reshape(flat) for a in (query_pre, key_pre, value_pre, grad_out)
    )
    partial = call(partial_body, struct((HEADS, LANES, LANES), BF16), key, value)
    value_rows = with_edges(value_pre).reshape((rows + 2) * cols, width)
    grad_rows = with_edges(grad_out).reshape((rows + 2) * cols, width)
    local, conv, taps_grad = call(
        lambda *refs: conv_body(rows, cols, *refs),
        (struct(flat, F32), struct(flat, F32), struct((9, width), F32)),
        value_rows,
        grad_rows,
        conv_taps.reshape(9, width),
    )
    for axis in ("space", "tm"):
        taps_grad = summed_over(taps_grad, axis)
    taps_grad = taps_grad.reshape(3, 3, width)
    state = scan_over(partial, merge_packed, False)
    attended, query_grad, grad_partial = call(
        forward_body,
        (struct(flat, BF16), struct(flat, BF16), struct((HEADS, HEAD_DIM, LANES), BF16)),
        query,
        grad,
        local,
        state,
    )
    grad_state = scan_over(grad_partial, add_packed, True)
    key_grad, value_grad = call(
        backward_body,
        (struct(flat, BF16), struct(flat, BF16)),
        key,
        value,
        conv,
        grad_state,
    )
    full = value_pre.shape
    return (
        attended.reshape(full),
        query_grad.reshape(full),
        key_grad.reshape(full),
        value_grad.reshape(full),
        taps_grad,
    )


def solution(mesh):
    tokens = P(("groups", "tm"), "space", None, None)
    return jax.shard_map(
        shards,
        mesh=mesh,
        in_specs=(tokens, tokens, tokens, tokens, P()),
        out_specs=(tokens, tokens, tokens, tokens, P("groups", None, None)),
        check_vma=False,
    )
```

```python
import functools

import jax
import jax.numpy as jnp
from jax import lax
from jax.experimental import pallas as pl
from jax.experimental.pallas import tpu as pltpu
from jax.sharding import PartitionSpec as P

HEADS = 20
HEAD_DIM = 112
LANES = 128
F32 = jnp.float32
BF16 = jnp.bfloat16
VMEM_LIMIT = 60 * 1024 * 1024


def cost(microseconds):
    return pl.CostEstimate(
        flops=int(microseconds * 1e9), bytes_accessed=int(microseconds * 3e6), transcendentals=0
    )


def call(body, out_shape, *args):
    return pl.pallas_call(
        body,
        out_shape=out_shape,
        in_specs=[pl.BlockSpec(memory_space=pltpu.VMEM)] * len(args),
        out_specs=jax.tree.map(lambda _: pl.BlockSpec(memory_space=pltpu.VMEM), out_shape),
        compiler_params=pltpu.CompilerParams(vmem_limit_bytes=VMEM_LIMIT),
        cost_estimate=cost(6),
    )(*args)


def struct(shape, dtype):
    return jax.ShapeDtypeStruct(shape, dtype)


def dot(a, b, dims):
    return lax.dot_general(a, b, (dims, ((), ())), preferred_element_type=F32)


def high_low(x):
    high = x.astype(BF16).astype(F32)
    return high, x - high


def conv_body(rows, cols, value_ref, grad_ref, edge_ref, taps_ref, local_ref, conv_ref, taps_grad_ref):
    width = value_ref.shape[1]
    count = rows * cols
    core = lax.axis_index("space")
    for low in range(0, width, LANES):
        lanes = slice(low, min(low + LANES, width))

        def banded(ref, which):
            edge = edge_ref[which, :, lanes].astype(F32)
            return jnp.concatenate(
                [
                    jnp.where(core == 1, edge, 0.0),
                    ref[:, lanes].astype(F32),
                    jnp.where(core == 0, edge, 0.0),
                ],
                axis=0,
            )

        value = banded(value_ref, 0)
        grad = banded(grad_ref, 1)
        col = lax.broadcasted_iota(jnp.int32, value.shape, 0) % cols
        total = value.shape[0]

        def left(x):
            return jnp.where(col == 0, 0.0, pltpu.roll(x, 1, 0))

        def right(x):
            return jnp.where(col == cols - 1, 0.0, pltpu.roll(x, total - 1, 0))

        values = (left(value), value, right(value))
        grads = (right(grad), grad, left(grad))
        centre = grad[cols : cols + count]
        local = conv = None
        for a in range(3):
            for b in range(3):
                tap = taps_ref[3 * a + b : 3 * a + b + 1, lanes]
                window = values[b][a * cols : a * cols + count]
                back = grads[b][(2 - a) * cols : (2 - a) * cols + count]
                local = tap * window if local is None else local + tap * window
                conv = tap * back if conv is None else conv + tap * back
                taps_grad_ref[3 * a + b : 3 * a + b + 1, lanes] = jnp.sum(
                    centre * window, axis=0, keepdims=True
                )
        local_ref[:, lanes] = local
        conv_ref[:, lanes] = conv


def guarded(x):
    return jnp.where(x > 0, 1.0 / jnp.where(x > 0, x, 1.0), 0.0)


def partial_body(key_ref, value_ref, out_ref):
    size = HEAD_DIM
    count = key_ref.shape[0]
    ones = jnp.where(
        lax.broadcasted_iota(jnp.int32, (count, LANES - size), 1) == 0, 1.0, 0.0
    ).astype(BF16)
    lane = lax.broadcasted_iota(jnp.int32, (size, LANES), 1)
    lane_row = lax.broadcasted_iota(jnp.int32, (1, LANES), 1)
    extra = lax.broadcasted_iota(jnp.int32, (LANES - size, LANES), 0)
    pad = jnp.zeros((1, LANES - size), F32)
    for head in range(HEADS):
        lanes = slice(head * size, (head + 1) * size)
        key = jnp.maximum(key_ref[:, lanes], 0)
        value = jnp.concatenate([value_ref[:, lanes], ones], axis=1)
        sums = dot(key, value, ((0,), (0,)))
        keys = sums[:, size : size + 1]
        inverse = guarded(jnp.sum(keys, axis=0, keepdims=True))
        mean = jnp.where(lane_row < size, jnp.sum(sums, axis=0, keepdims=True) * inverse, 0.0)
        keys_row = jnp.concatenate(
            [jnp.sum(key.astype(F32), axis=0, keepdims=True), pad], axis=1
        )
        out_ref[head] = join(sums - keys * mean, keys, keys_row, mean, lane, extra).astype(BF16)


def join(centred, keys, keys_row, mean, lane, extra):
    size = HEAD_DIM
    high, low = high_low(keys)
    top = jnp.where(
        lane < size, centred, jnp.where(lane == size, high, jnp.where(lane == size + 1, low, 0.0))
    )
    mean_high, mean_low = high_low(mean)
    row_high, row_low = high_low(keys_row)
    bottom = jnp.where(
        extra == 0,
        mean_high,
        jnp.where(extra == 1, mean_low, jnp.where(extra == 2, row_high, jnp.where(extra == 3, row_low, 0.0))),
    )
    return jnp.concatenate([top, bottom], axis=0)


def parts_of(packed):
    size = HEAD_DIM
    top = packed[:size]
    keys = top[:, size : size + 1] + top[:, size + 1 : size + 2]
    mean = packed[size : size + 1] + packed[size + 1 : size + 2]
    keys_row = packed[size + 2 : size + 3] + packed[size + 3 : size + 4]
    return top, keys, keys_row, mean


def merge_packed(first, second, lane, extra):
    top_a, keys_a, row_a, mean_a = parts_of(first)
    top_b, keys_b, row_b, mean_b = parts_of(second)
    mass_a = jnp.sum(keys_a, axis=0, keepdims=True)
    mass_b = jnp.sum(keys_b, axis=0, keepdims=True)
    mean = (mass_a * mean_a + mass_b * mean_b) * guarded(mass_a + mass_b)
    centred = top_a + top_b + keys_a * (mean_a - mean) + keys_b * (mean_b - mean)
    return join(centred, keys_a + keys_b, row_a + row_b, mean, lane, extra)


def add_packed(first, second, lane, extra):
    size = HEAD_DIM
    merged = first + second
    sums = merged[:, size : size + 1] + merged[:, size + 1 : size + 2]
    high, low = high_low(sums)
    return jnp.where(
        lane < size, merged, jnp.where(lane == size, high, jnp.where(lane == size + 1, low, 0.0))
    )


def scan_body(
    merge,
    reverse,
    local_ref,
    out_ref,
    half_ref,
    both_ref,
    core_recv,
    pair_send,
    pair_recv,
    chain_send,
    chain_recv,
    core_sems,
    pair_sems,
    chain_sems,
    out_sems,
):
    heads = core_recv.shape[0]
    core = lax.axis_index("space")
    place = lax.axis_index("tm")
    links = lax.axis_size("tm") // 2
    link, side = place // 2, place % 2
    pair = link * 2 + (1 - side)
    if reverse:
        order, ahead, behind, sums_both = links - 1 - link, place - 2, place + 2, side == 0
    else:
        order, ahead, behind, sums_both = link, place + 2, place - 2, side == 1
    lane = lax.broadcasted_iota(jnp.int32, (HEAD_DIM, LANES), 1)
    extra = lax.broadcasted_iota(jnp.int32, (LANES - HEAD_DIM, LANES), 0)

    def remote(source, target, sems, head, device):
        return pltpu.make_async_remote_copy(
            src_ref=source,
            dst_ref=target,
            send_sem=sems.at[0, head],
            recv_sem=sems.at[1, head],
            device_id=device,
            device_id_type=pl.DeviceIdType.MESH,
        )

    def core_copy(head):
        return remote(
            local_ref.at[(1 - core) * heads + head],
            core_recv.at[head],
            core_sems,
            head,
            {"space": 1 - core},
        )

    def pair_copy(head):
        return remote(pair_send.at[head], pair_recv.at[head], pair_sems, head, {"tm": pair})

    def chain_copy(head):
        return remote(chain_send.at[head], chain_recv.at[head], chain_sems, head, {"tm": ahead})

    def out_copy(head):
        mine = out_ref.at[core * heads + head]
        return remote(mine, mine, out_sems, head, {"space": 1 - core})

    barrier = pltpu.get_barrier_semaphore()

    def greet(device):
        pl.semaphore_signal(barrier, inc=1, device_id=device, device_id_type=pl.DeviceIdType.MESH)

    greet({"space": 1 - core})
    greet({"tm": pair})

    @pl.when(order < links - 1)
    def _():
        greet({"tm": ahead})

    @pl.when(order > 0)
    def _():
        greet({"tm": behind})

    peers = 2 + jnp.minimum(order, 1) + jnp.minimum(links - 1 - order, 1)
    pl.semaphore_wait(barrier, peers)

    def begin(head, _):
        core_copy(head).start()
        return 0

    lax.fori_loop(0, heads, begin, 0)

    def over_cores(head, _):
        core_copy(head).wait_recv()
        half = merge(
            local_ref[core * heads + head].astype(F32), core_recv[head].astype(F32), lane, extra
        )
        half_ref[head] = half
        pair_send[head] = half.astype(BF16)
        pair_copy(head).start()
        return 0

    lax.fori_loop(0, heads, over_cores, 0)

    def give(head, total):
        out_ref[core * heads + head] = total.astype(BF16)
        out_copy(head).start()

    def over_pairs(head, _):
        pair_copy(head).wait_recv()
        half = half_ref[head]
        both = merge(half, pair_recv[head].astype(F32), lane, extra)
        both_ref[head] = both

        @pl.when(order == 0)
        def _():
            @pl.when(order < links - 1)
            def _():
                chain_send[head] = both.astype(BF16)
                chain_copy(head).start()

            give(head, jnp.where(sums_both, both, half))

        return 0

    lax.fori_loop(0, heads, over_pairs, 0)

    @pl.when(order > 0)
    def _():
        def over_chain(head, _):
            both = both_ref[head]
            chain_copy(head).wait_recv()
            before = chain_recv[head].astype(F32)

            @pl.when(order < links - 1)
            def _():
                chain_send[head] = merge(before, both, lane, extra).astype(BF16)
                chain_copy(head).start()

            mine = jnp.where(sums_both, both, half_ref[head])
            give(head, merge(before, mine, lane, extra))
            return 0

        lax.fori_loop(0, heads, over_chain, 0)

    def finish(head, _):
        core_copy(head).wait_send()
        pair_copy(head).wait_send()

        @pl.when(order < links - 1)
        def _():
            chain_copy(head).wait_send()

        out_copy(head).wait()
        return 0

    lax.fori_loop(0, heads, finish, 0)


def forward_body(query_ref, grad_ref, local_ref, state_ref, attended_ref, query_grad_ref, out_ref):
    size = HEAD_DIM
    count = query_ref.shape[0]
    lane = lax.broadcasted_iota(jnp.int32, (size, LANES), 1)
    tail = lax.broadcasted_iota(jnp.int32, (count, LANES - size), 1)
    for head in range(HEADS):
        lanes = slice(head * size, (head + 1) * size)
        query_pre = query_ref[:, lanes]
        query = jnp.maximum(query_pre, 0)
        grad = grad_ref[:, lanes]
        cotangent = grad.astype(F32)
        state = state_ref[head]
        mixed = dot(query, state[:size], ((1,), (0,)))
        back = dot(grad, state[:, :size], ((1,), (1,)))
        centred = mixed[:, :size]
        mass = mixed[:, size : size + 1] + mixed[:, size + 1 : size + 2]
        inverse = 1.0 / (mass + 1.0)
        rows = state[size:].astype(F32)
        mean = rows[0:1, :size] + rows[1:2, :size]
        keys_row = rows[2:3, :size] + rows[3:4, :size]
        output = (centred + mass * mean) * inverse
        attended_ref[:, lanes] = (output + local_ref[:, lanes]).astype(BF16)
        along = back[:, size : size + 1] + back[:, size + 1 : size + 2]
        product = jnp.sum(cotangent * centred, axis=1, keepdims=True)
        grad_query = (back[:, :size] + ((along - product) * inverse) * keys_row) * inverse
        query_grad_ref[:, lanes] = jnp.where(
            query_pre.astype(F32) > 0, grad_query, 0.0
        ).astype(BF16)
        high, low = high_low(-(product + mass * along) * inverse)
        side = jnp.where(tail == 0, high, jnp.where(tail == 1, low, 0.0)).astype(BF16)
        scaled = (query.astype(F32) * inverse).astype(BF16)
        sums = dot(scaled, jnp.concatenate([grad, side], axis=1), ((0,), (0,)))
        total = sums[:, size : size + 1] + sums[:, size + 1 : size + 2]
        high, low = high_low(total)
        out_ref[head] = jnp.where(
            lane < size, sums, jnp.where(lane == size, high, jnp.where(lane == size + 1, low, 0.0))
        ).astype(BF16)


def backward_body(key_ref, value_ref, conv_ref, state_ref, key_grad_ref, value_grad_ref):
    size = HEAD_DIM
    count = key_ref.shape[0]
    ones = jnp.where(
        lax.broadcasted_iota(jnp.int32, (count, LANES - size), 1) < 2, 1.0, 0.0
    ).astype(BF16)
    for head in range(HEADS):
        lanes = slice(head * size, (head + 1) * size)
        key_pre = key_ref[:, lanes]
        state = state_ref[head]
        value = jnp.concatenate([value_ref[:, lanes], ones], axis=1)
        grad_key = dot(value, state, ((1,), (1,)))
        mixed = dot(jnp.maximum(key_pre, 0), state, ((1,), (0,)))
        key_grad_ref[:, lanes] = jnp.where(key_pre.astype(F32) > 0, grad_key, 0.0).astype(BF16)
        value_grad_ref[:, lanes] = (mixed[:, :size] + conv_ref[:, lanes]).astype(BF16)


def edge_rows(*blocks):
    place = lax.axis_index("space")
    last = blocks[0].shape[1] - 1
    own = jnp.stack(
        [lax.dynamic_index_in_dim(a[0], (1 - place) * last, 0, False) for a in blocks]
    )
    return lax.ppermute(own, "space", [(0, 1), (1, 0)])


def scan_over(local, merge, reverse):
    half = (local.shape[0] // 2,) + local.shape[1:]
    sems = pltpu.SemaphoreType.DMA((2, half[0]))
    return pl.pallas_call(
        functools.partial(scan_body, merge, reverse),
        out_shape=struct(local.shape, BF16),
        in_specs=[pl.BlockSpec(memory_space=pltpu.VMEM)],
        out_specs=pl.BlockSpec(memory_space=pltpu.VMEM),
        scratch_shapes=[pltpu.VMEM(half, F32)] * 2 + [pltpu.VMEM(half, BF16)] * 5 + [sems] * 4,
        compiler_params=pltpu.CompilerParams(
            collective_id=int(reverse), has_side_effects=True, vmem_limit_bytes=VMEM_LIMIT
        ),
        cost_estimate=cost(25),
    )(local)


def summed_over(x, axis):
    count = lax.axis_size(axis)
    if count & (count - 1):
        return lax.psum(x, axis)
    step = 1
    while step < count:
        x = x + lax.ppermute(x, axis, [(i, i ^ step) for i in range(count)])
        step *= 2
    return x


def shards(query_pre, key_pre, value_pre, grad_out, conv_taps):
    frames, rows, cols, width = value_pre.shape
    assert frames == 1 and width == HEADS * HEAD_DIM and lax.axis_size("space") == 2
    assert lax.axis_size("tm") % 2 == 0
    count = rows * cols
    flat = (count, width)
    query, key, value, grad = (
        a.reshape(flat) for a in (query_pre, key_pre, value_pre, grad_out)
    )
    partial = call(partial_body, struct((HEADS, LANES, LANES), BF16), key, value)
    edges = edge_rows(value_pre, grad_out)
    local, conv, taps_grad = call(
        lambda *refs: conv_body(rows, cols, *refs),
        (struct(flat, F32), struct(flat, F32), struct((9, width), F32)),
        value,
        grad,
        edges,
        conv_taps.reshape(9, width),
    )
    for axis in ("space", "tm"):
        taps_grad = summed_over(taps_grad, axis)
    taps_grad = taps_grad.reshape(3, 3, width)
    state = scan_over(partial, merge_packed, False)
    attended, query_grad, grad_partial = call(
        forward_body,
        (struct(flat, BF16), struct(flat, BF16), struct((HEADS, HEAD_DIM, LANES), BF16)),
        query,
        grad,
        local,
        state,
    )
    grad_state = scan_over(grad_partial, add_packed, True)
    key_grad, value_grad = call(
        backward_body,
        (struct(flat, BF16), struct(flat, BF16)),
        key,
        value,
        conv,
        grad_state,
    )
    full = value_pre.shape
    return (
        attended.reshape(full),
        query_grad.reshape(full),
        key_grad.reshape(full),
        value_grad.reshape(full),
        taps_grad,
    )


def solution(mesh):
    tokens = P(("groups", "tm"), "space", None, None)
    return jax.shard_map(
        shards,
        mesh=mesh,
        in_specs=(tokens, tokens, tokens, tokens, P()),
        out_specs=(tokens, tokens, tokens, tokens, P("groups", None, None)),
        check_vma=False,
    )
```

```python
import functools

import jax
import jax.numpy as jnp
from jax import lax
from jax.experimental import pallas as pl
from jax.experimental.pallas import tpu as pltpu
from jax.sharding import PartitionSpec as P

HEADS = 20
HEAD_DIM = 112
LANES = 128
F32 = jnp.float32
BF16 = jnp.bfloat16
VMEM_LIMIT = 60 * 1024 * 1024


def cost(microseconds):
    return pl.CostEstimate(
        flops=int(microseconds * 1e9), bytes_accessed=int(microseconds * 3e6), transcendentals=0
    )


def call(body, out_shape, *args):
    return pl.pallas_call(
        body,
        out_shape=out_shape,
        in_specs=[pl.BlockSpec(memory_space=pltpu.VMEM)] * len(args),
        out_specs=jax.tree.map(lambda _: pl.BlockSpec(memory_space=pltpu.VMEM), out_shape),
        compiler_params=pltpu.CompilerParams(vmem_limit_bytes=VMEM_LIMIT),
        cost_estimate=cost(6),
    )(*args)


def struct(shape, dtype):
    return jax.ShapeDtypeStruct(shape, dtype)


def dot(a, b, dims):
    return lax.dot_general(a, b, (dims, ((), ())), preferred_element_type=F32)


def high_low(x):
    high = x.astype(BF16).astype(F32)
    return high, x - high


def conv_body(rows, cols, value_ref, grad_ref, edge_ref, taps_ref, local_ref, conv_ref, taps_grad_ref):
    width = value_ref.shape[1]
    count = rows * cols
    core = lax.axis_index("space")
    for low in range(0, width, LANES):
        lanes = slice(low, min(low + LANES, width))

        def banded(ref, which):
            edge = edge_ref[which, :, lanes].astype(F32)
            return jnp.concatenate(
                [
                    jnp.where(core == 1, edge, 0.0),
                    ref[:, lanes].astype(F32),
                    jnp.where(core == 0, edge, 0.0),
                ],
                axis=0,
            )

        value = banded(value_ref, 0)
        grad = banded(grad_ref, 1)
        col = lax.broadcasted_iota(jnp.int32, value.shape, 0) % cols
        total = value.shape[0]

        def left(x):
            return jnp.where(col == 0, 0.0, pltpu.roll(x, 1, 0))

        def right(x):
            return jnp.where(col == cols - 1, 0.0, pltpu.roll(x, total - 1, 0))

        values = (left(value), value, right(value))
        grads = (right(grad), grad, left(grad))
        centre = grad[cols : cols + count]
        local = conv = None
        for a in range(3):
            for b in range(3):
                tap = taps_ref[3 * a + b : 3 * a + b + 1, lanes]
                window = values[b][a * cols : a * cols + count]
                back = grads[b][(2 - a) * cols : (2 - a) * cols + count]
                local = tap * window if local is None else local + tap * window
                conv = tap * back if conv is None else conv + tap * back
                taps_grad_ref[3 * a + b : 3 * a + b + 1, lanes] = jnp.sum(
                    centre * window, axis=0, keepdims=True
                )
        local_ref[:, lanes] = local
        conv_ref[:, lanes] = conv


def guarded(x):
    return jnp.where(x > 0, 1.0 / jnp.where(x > 0, x, 1.0), 0.0)


def partial_body(key_ref, value_ref, out_ref):
    size = HEAD_DIM
    count = key_ref.shape[0]
    ones = jnp.where(
        lax.broadcasted_iota(jnp.int32, (count, LANES - size), 1) == 0, 1.0, 0.0
    ).astype(BF16)
    lane = lax.broadcasted_iota(jnp.int32, (size, LANES), 1)
    lane_row = lax.broadcasted_iota(jnp.int32, (1, LANES), 1)
    extra = lax.broadcasted_iota(jnp.int32, (LANES - size, LANES), 0)
    pad = jnp.zeros((1, LANES - size), F32)
    for head in range(HEADS):
        lanes = slice(head * size, (head + 1) * size)
        key = jnp.maximum(key_ref[:, lanes], 0)
        value = jnp.concatenate([value_ref[:, lanes], ones], axis=1)
        sums = dot(key, value, ((0,), (0,)))
        keys = sums[:, size : size + 1]
        inverse = guarded(jnp.sum(keys, axis=0, keepdims=True))
        mean = jnp.where(lane_row < size, jnp.sum(sums, axis=0, keepdims=True) * inverse, 0.0)
        keys_row = jnp.concatenate(
            [jnp.sum(key.astype(F32), axis=0, keepdims=True), pad], axis=1
        )
        out_ref[head] = join(sums - keys * mean, keys, keys_row, mean, lane, extra).astype(BF16)


def join(centred, keys, keys_row, mean, lane, extra):
    size = HEAD_DIM
    high, low = high_low(keys)
    top = jnp.where(
        lane < size, centred, jnp.where(lane == size, high, jnp.where(lane == size + 1, low, 0.0))
    )
    mean_high, mean_low = high_low(mean)
    row_high, row_low = high_low(keys_row)
    bottom = jnp.where(
        extra == 0,
        mean_high,
        jnp.where(extra == 1, mean_low, jnp.where(extra == 2, row_high, jnp.where(extra == 3, row_low, 0.0))),
    )
    return jnp.concatenate([top, bottom], axis=0)


def parts_of(packed):
    size = HEAD_DIM
    top = packed[:size]
    keys = top[:, size : size + 1] + top[:, size + 1 : size + 2]
    mean = packed[size : size + 1] + packed[size + 1 : size + 2]
    keys_row = packed[size + 2 : size + 3] + packed[size + 3 : size + 4]
    return top, keys, keys_row, mean


def merge_packed(first, second, lane, extra):
    top_a, keys_a, row_a, mean_a = parts_of(first)
    top_b, keys_b, row_b, mean_b = parts_of(second)
    mass_a = jnp.sum(keys_a, axis=0, keepdims=True)
    mass_b = jnp.sum(keys_b, axis=0, keepdims=True)
    mean = (mass_a * mean_a + mass_b * mean_b) * guarded(mass_a + mass_b)
    centred = top_a + top_b + keys_a * (mean_a - mean) + keys_b * (mean_b - mean)
    return join(centred, keys_a + keys_b, row_a + row_b, mean, lane, extra)


def add_packed(first, second, lane, extra):
    size = HEAD_DIM
    merged = first + second
    sums = merged[:, size : size + 1] + merged[:, size + 1 : size + 2]
    high, low = high_low(sums)
    return jnp.where(
        lane < size, merged, jnp.where(lane == size, high, jnp.where(lane == size + 1, low, 0.0))
    )


def scan_body(
    merge,
    reverse,
    local_ref,
    out_ref,
    half_ref,
    both_ref,
    core_recv,
    pair_send,
    pair_recv,
    chain_send,
    chain_recv,
    core_sems,
    pair_sems,
    chain_sems,
    out_sems,
):
    heads = core_recv.shape[0]
    core = lax.axis_index("space")
    place = lax.axis_index("tm")
    links = lax.axis_size("tm") // 2
    link, side = place // 2, place % 2
    pair = link * 2 + (1 - side)
    if reverse:
        order, ahead, behind, sums_both = links - 1 - link, place - 2, place + 2, side == 0
    else:
        order, ahead, behind, sums_both = link, place + 2, place - 2, side == 1
    lane = lax.broadcasted_iota(jnp.int32, (HEAD_DIM, LANES), 1)
    extra = lax.broadcasted_iota(jnp.int32, (LANES - HEAD_DIM, LANES), 0)

    def remote(source, target, sems, head, device):
        return pltpu.make_async_remote_copy(
            src_ref=source,
            dst_ref=target,
            send_sem=sems.at[0, head],
            recv_sem=sems.at[1, head],
            device_id=device,
            device_id_type=pl.DeviceIdType.MESH,
        )

    def core_copy(head):
        return remote(
            local_ref.at[(1 - core) * heads + head],
            core_recv.at[head],
            core_sems,
            head,
            {"space": 1 - core},
        )

    def pair_copy(head):
        return remote(pair_send.at[head], pair_recv.at[head], pair_sems, head, {"tm": pair})

    def chain_copy(head):
        return remote(chain_send.at[head], chain_recv.at[head], chain_sems, head, {"tm": ahead})

    def out_copy(head):
        mine = out_ref.at[core * heads + head]
        return remote(mine, mine, out_sems, head, {"space": 1 - core})

    barrier = pltpu.get_barrier_semaphore()

    def greet(device):
        pl.semaphore_signal(barrier, inc=1, device_id=device, device_id_type=pl.DeviceIdType.MESH)

    greet({"space": 1 - core})
    greet({"tm": pair})

    @pl.when(order < links - 1)
    def _():
        greet({"tm": ahead})

    @pl.when(order > 0)
    def _():
        greet({"tm": behind})

    peers = 2 + jnp.minimum(order, 1) + jnp.minimum(links - 1 - order, 1)
    pl.semaphore_wait(barrier, peers)

    def begin(head, _):
        core_copy(head).start()
        return 0

    lax.fori_loop(0, heads, begin, 0)

    group = 2 if heads % 2 == 0 else 1

    def over_cores(turn, _):
        batch = [turn * group + i for i in range(group)]
        for head in batch:
            core_copy(head).wait_recv()
        halves = [
            merge(
                local_ref[core * heads + head].astype(F32),
                core_recv[head].astype(F32),
                lane,
                extra,
            )
            for head in batch
        ]
        for head, half in zip(batch, halves):
            half_ref[head] = half
            pair_send[head] = half.astype(BF16)
        for head in batch:
            pair_copy(head).start()
        return 0

    lax.fori_loop(0, heads // group, over_cores, 0)

    def give(head, total):
        out_ref[core * heads + head] = total.astype(BF16)
        out_copy(head).start()

    def over_pairs(turn, _):
        batch = [turn * group + i for i in range(group)]
        for head in batch:
            pair_copy(head).wait_recv()
        halves = [half_ref[head] for head in batch]
        boths = [
            merge(half, pair_recv[head].astype(F32), lane, extra)
            for head, half in zip(batch, halves)
        ]
        for head, both in zip(batch, boths):
            both_ref[head] = both

        @pl.when(order == 0)
        def _():
            @pl.when(order < links - 1)
            def _():
                for head, both in zip(batch, boths):
                    chain_send[head] = both.astype(BF16)
                    chain_copy(head).start()

            for head, half, both in zip(batch, halves, boths):
                give(head, jnp.where(sums_both, both, half))

        return 0

    lax.fori_loop(0, heads // group, over_pairs, 0)

    @pl.when(order > 0)
    def _():
        def over_chain(head, _):
            both = both_ref[head]
            chain_copy(head).wait_recv()
            before = chain_recv[head].astype(F32)

            @pl.when(order < links - 1)
            def _():
                chain_send[head] = merge(before, both, lane, extra).astype(BF16)
                chain_copy(head).start()

            mine = jnp.where(sums_both, both, half_ref[head])
            give(head, merge(before, mine, lane, extra))
            return 0

        lax.fori_loop(0, heads, over_chain, 0)

    def finish(head, _):
        core_copy(head).wait_send()
        pair_copy(head).wait_send()

        @pl.when(order < links - 1)
        def _():
            chain_copy(head).wait_send()

        out_copy(head).wait()
        return 0

    lax.fori_loop(0, heads, finish, 0)


def forward_body(query_ref, grad_ref, local_ref, state_ref, attended_ref, query_grad_ref, out_ref):
    size = HEAD_DIM
    count = query_ref.shape[0]
    lane = lax.broadcasted_iota(jnp.int32, (size, LANES), 1)
    tail = lax.broadcasted_iota(jnp.int32, (count, LANES - size), 1)
    for head in range(HEADS):
        lanes = slice(head * size, (head + 1) * size)
        query_pre = query_ref[:, lanes]
        query = jnp.maximum(query_pre, 0)
        grad = grad_ref[:, lanes]
        cotangent = grad.astype(F32)
        state = state_ref[head]
        mixed = dot(query, state[:size], ((1,), (0,)))
        back = dot(grad, state[:, :size], ((1,), (1,)))
        centred = mixed[:, :size]
        mass = mixed[:, size : size + 1] + mixed[:, size + 1 : size + 2]
        inverse = 1.0 / (mass + 1.0)
        rows = state[size:].astype(F32)
        mean = rows[0:1, :size] + rows[1:2, :size]
        keys_row = rows[2:3, :size] + rows[3:4, :size]
        output = (centred + mass * mean) * inverse
        attended_ref[:, lanes] = (output + local_ref[:, lanes]).astype(BF16)
        along = back[:, size : size + 1] + back[:, size + 1 : size + 2]
        product = jnp.sum(cotangent * centred, axis=1, keepdims=True)
        grad_query = (back[:, :size] + ((along - product) * inverse) * keys_row) * inverse
        query_grad_ref[:, lanes] = jnp.where(
            query_pre.astype(F32) > 0, grad_query, 0.0
        ).astype(BF16)
        high, low = high_low(-(product + mass * along) * inverse)
        side = jnp.where(tail == 0, high, jnp.where(tail == 1, low, 0.0)).astype(BF16)
        scaled = (query.astype(F32) * inverse).astype(BF16)
        sums = dot(scaled, jnp.concatenate([grad, side], axis=1), ((0,), (0,)))
        total = sums[:, size : size + 1] + sums[:, size + 1 : size + 2]
        high, low = high_low(total)
        out_ref[head] = jnp.where(
            lane < size, sums, jnp.where(lane == size, high, jnp.where(lane == size + 1, low, 0.0))
        ).astype(BF16)


def backward_body(key_ref, value_ref, conv_ref, state_ref, key_grad_ref, value_grad_ref):
    size = HEAD_DIM
    count = key_ref.shape[0]
    ones = jnp.where(
        lax.broadcasted_iota(jnp.int32, (count, LANES - size), 1) < 2, 1.0, 0.0
    ).astype(BF16)
    for head in range(HEADS):
        lanes = slice(head * size, (head + 1) * size)
        key_pre = key_ref[:, lanes]
        state = state_ref[head]
        value = jnp.concatenate([value_ref[:, lanes], ones], axis=1)
        grad_key = dot(value, state, ((1,), (1,)))
        mixed = dot(jnp.maximum(key_pre, 0), state, ((1,), (0,)))
        key_grad_ref[:, lanes] = jnp.where(key_pre.astype(F32) > 0, grad_key, 0.0).astype(BF16)
        value_grad_ref[:, lanes] = (mixed[:, :size] + conv_ref[:, lanes]).astype(BF16)


def edge_rows(*blocks):
    place = lax.axis_index("space")
    last = blocks[0].shape[1] - 1
    own = jnp.stack(
        [lax.dynamic_index_in_dim(a[0], (1 - place) * last, 0, False) for a in blocks]
    )
    return lax.ppermute(own, "space", [(0, 1), (1, 0)])


def scan_over(local, merge, reverse):
    half = (local.shape[0] // 2,) + local.shape[1:]
    sems = pltpu.SemaphoreType.DMA((2, half[0]))
    return pl.pallas_call(
        functools.partial(scan_body, merge, reverse),
        out_shape=struct(local.shape, BF16),
        in_specs=[pl.BlockSpec(memory_space=pltpu.VMEM)],
        out_specs=pl.BlockSpec(memory_space=pltpu.VMEM),
        scratch_shapes=[pltpu.VMEM(half, F32)] * 2 + [pltpu.VMEM(half, BF16)] * 5 + [sems] * 4,
        compiler_params=pltpu.CompilerParams(
            collective_id=int(reverse), has_side_effects=True, vmem_limit_bytes=VMEM_LIMIT
        ),
        cost_estimate=cost(25),
    )(local)


def summed_over(x, axis):
    count = lax.axis_size(axis)
    if count & (count - 1):
        return lax.psum(x, axis)
    step = 1
    while step < count:
        x = x + lax.ppermute(x, axis, [(i, i ^ step) for i in range(count)])
        step *= 2
    return x


def shards(query_pre, key_pre, value_pre, grad_out, conv_taps):
    frames, rows, cols, width = value_pre.shape
    assert frames == 1 and width == HEADS * HEAD_DIM and lax.axis_size("space") == 2
    assert lax.axis_size("tm") % 2 == 0
    count = rows * cols
    flat = (count, width)
    query, key, value, grad = (
        a.reshape(flat) for a in (query_pre, key_pre, value_pre, grad_out)
    )
    partial = call(partial_body, struct((HEADS, LANES, LANES), BF16), key, value)
    edges = edge_rows(value_pre, grad_out)
    local, conv, taps_grad = call(
        lambda *refs: conv_body(rows, cols, *refs),
        (struct(flat, F32), struct(flat, F32), struct((9, width), F32)),
        value,
        grad,
        edges,
        conv_taps.reshape(9, width),
    )
    for axis in ("space", "tm"):
        taps_grad = summed_over(taps_grad, axis)
    taps_grad = taps_grad.reshape(3, 3, width)
    state = scan_over(partial, merge_packed, False)
    attended, query_grad, grad_partial = call(
        forward_body,
        (struct(flat, BF16), struct(flat, BF16), struct((HEADS, HEAD_DIM, LANES), BF16)),
        query,
        grad,
        local,
        state,
    )
    grad_state = scan_over(grad_partial, add_packed, True)
    key_grad, value_grad = call(
        backward_body,
        (struct(flat, BF16), struct(flat, BF16)),
        key,
        value,
        conv,
        grad_state,
    )
    full = value_pre.shape
    return (
        attended.reshape(full),
        query_grad.reshape(full),
        key_grad.reshape(full),
        value_grad.reshape(full),
        taps_grad,
    )


def solution(mesh):
    tokens = P(("groups", "tm"), "space", None, None)
    return jax.shard_map(
        shards,
        mesh=mesh,
        in_specs=(tokens, tokens, tokens, tokens, P()),
        out_specs=(tokens, tokens, tokens, tokens, P("groups", None, None)),
        check_vma=False,
    )
```

```python
import functools

import jax
import jax.numpy as jnp
from jax import lax
from jax.experimental import pallas as pl
from jax.experimental.pallas import tpu as pltpu
from jax.sharding import PartitionSpec as P

HEADS = 20
HEAD_DIM = 112
LANES = 128
F32 = jnp.float32
BF16 = jnp.bfloat16
VMEM_LIMIT = 60 * 1024 * 1024


def cost(microseconds):
    return pl.CostEstimate(
        flops=int(microseconds * 1e9), bytes_accessed=int(microseconds * 3e6), transcendentals=0
    )


def call(body, out_shape, *args):
    return pl.pallas_call(
        body,
        out_shape=out_shape,
        in_specs=[pl.BlockSpec(memory_space=pltpu.VMEM)] * len(args),
        out_specs=jax.tree.map(lambda _: pl.BlockSpec(memory_space=pltpu.VMEM), out_shape),
        compiler_params=pltpu.CompilerParams(vmem_limit_bytes=VMEM_LIMIT),
        cost_estimate=cost(6),
    )(*args)


def struct(shape, dtype):
    return jax.ShapeDtypeStruct(shape, dtype)


def dot(a, b, dims):
    return lax.dot_general(a, b, (dims, ((), ())), preferred_element_type=F32)


def high_low(x):
    high = x.astype(BF16).astype(F32)
    return high, x - high


def conv_body(rows, cols, value_ref, grad_ref, edge_ref, taps_ref, local_ref, conv_ref, taps_grad_ref):
    width = value_ref.shape[1]
    count = rows * cols
    core = lax.axis_index("space")
    for low in range(0, width, LANES):
        lanes = slice(low, min(low + LANES, width))

        def banded(ref, which):
            edge = edge_ref[which, :, lanes].astype(F32)
            return jnp.concatenate(
                [
                    jnp.where(core == 1, edge, 0.0),
                    ref[:, lanes].astype(F32),
                    jnp.where(core == 0, edge, 0.0),
                ],
                axis=0,
            )

        value = banded(value_ref, 0)
        grad = banded(grad_ref, 1)
        col = lax.broadcasted_iota(jnp.int32, value.shape, 0) % cols
        total = value.shape[0]

        def left(x):
            return jnp.where(col == 0, 0.0, pltpu.roll(x, 1, 0))

        def right(x):
            return jnp.where(col == cols - 1, 0.0, pltpu.roll(x, total - 1, 0))

        values = (left(value), value, right(value))
        grads = (right(grad), grad, left(grad))
        centre = grad[cols : cols + count]
        local = conv = None
        for a in range(3):
            for b in range(3):
                tap = taps_ref[3 * a + b : 3 * a + b + 1, lanes]
                window = values[b][a * cols : a * cols + count]
                back = grads[b][(2 - a) * cols : (2 - a) * cols + count]
                local = tap * window if local is None else local + tap * window
                conv = tap * back if conv is None else conv + tap * back
                taps_grad_ref[3 * a + b : 3 * a + b + 1, lanes] = jnp.sum(
                    centre * window, axis=0, keepdims=True
                )
        local_ref[:, lanes] = local
        conv_ref[:, lanes] = conv


def guarded(x):
    return jnp.where(x > 0, 1.0 / jnp.where(x > 0, x, 1.0), 0.0)


def partial_body(key_ref, value_ref, out_ref):
    size = HEAD_DIM
    count = key_ref.shape[0]
    ones = jnp.where(
        lax.broadcasted_iota(jnp.int32, (count, LANES - size), 1) == 0, 1.0, 0.0
    ).astype(BF16)
    lane = lax.broadcasted_iota(jnp.int32, (size, LANES), 1)
    lane_row = lax.broadcasted_iota(jnp.int32, (1, LANES), 1)
    extra = lax.broadcasted_iota(jnp.int32, (LANES - size, LANES), 0)
    pad = jnp.zeros((1, LANES - size), F32)
    for head in range(HEADS):
        lanes = slice(head * size, (head + 1) * size)
        key = jnp.maximum(key_ref[:, lanes], 0)
        value = jnp.concatenate([value_ref[:, lanes], ones], axis=1)
        sums = dot(key, value, ((0,), (0,)))
        keys = sums[:, size : size + 1]
        inverse = guarded(jnp.sum(keys, axis=0, keepdims=True))
        mean = jnp.where(lane_row < size, jnp.sum(sums, axis=0, keepdims=True) * inverse, 0.0)
        keys_row = jnp.concatenate(
            [jnp.sum(key.astype(F32), axis=0, keepdims=True), pad], axis=1
        )
        out_ref[head] = join(sums - keys * mean, keys, keys_row, mean, lane, extra).astype(BF16)


def join(centred, keys, keys_row, mean, lane, extra):
    size = HEAD_DIM
    high, low = high_low(keys)
    top = jnp.where(
        lane < size, centred, jnp.where(lane == size, high, jnp.where(lane == size + 1, low, 0.0))
    )
    mean_high, mean_low = high_low(mean)
    row_high, row_low = high_low(keys_row)
    bottom = jnp.where(
        extra == 0,
        mean_high,
        jnp.where(extra == 1, mean_low, jnp.where(extra == 2, row_high, jnp.where(extra == 3, row_low, 0.0))),
    )
    return jnp.concatenate([top, bottom], axis=0)


def parts_of(packed):
    size = HEAD_DIM
    top = packed[:size]
    keys = top[:, size : size + 1] + top[:, size + 1 : size + 2]
    mean = packed[size : size + 1] + packed[size + 1 : size + 2]
    keys_row = packed[size + 2 : size + 3] + packed[size + 3 : size + 4]
    return top, keys, keys_row, mean


def merge_packed(first, second, lane, extra):
    top_a, keys_a, row_a, mean_a = parts_of(first)
    top_b, keys_b, row_b, mean_b = parts_of(second)
    mass_a = jnp.sum(keys_a, axis=0, keepdims=True)
    mass_b = jnp.sum(keys_b, axis=0, keepdims=True)
    mean = (mass_a * mean_a + mass_b * mean_b) * guarded(mass_a + mass_b)
    centred = top_a + top_b + keys_a * (mean_a - mean) + keys_b * (mean_b - mean)
    return join(centred, keys_a + keys_b, row_a + row_b, mean, lane, extra)


def add_packed(first, second, lane, extra):
    size = HEAD_DIM
    merged = first + second
    sums = merged[:, size : size + 1] + merged[:, size + 1 : size + 2]
    high, low = high_low(sums)
    return jnp.where(
        lane < size, merged, jnp.where(lane == size, high, jnp.where(lane == size + 1, low, 0.0))
    )


def scan_body(
    merge,
    reverse,
    work,
    inputs,
    *refs,
):
    local_ref, out_ref = refs[0], refs[1 + inputs]
    work_refs = refs[1 : 1 + inputs] + refs[2 + inputs : -11]
    (
    half_ref,
    both_ref,
    core_recv,
    pair_send,
    pair_recv,
    chain_send,
    chain_recv,
    core_sems,
    pair_sems,
    chain_sems,
    out_sems,
    ) = refs[-11:]
    heads = core_recv.shape[0]
    core = lax.axis_index("space")
    place = lax.axis_index("tm")
    links = lax.axis_size("tm") // 2
    link, side = place // 2, place % 2
    pair = link * 2 + (1 - side)
    if reverse:
        order, ahead, behind, sums_both = links - 1 - link, place - 2, place + 2, side == 0
    else:
        order, ahead, behind, sums_both = link, place + 2, place - 2, side == 1
    lane = lax.broadcasted_iota(jnp.int32, (HEAD_DIM, LANES), 1)
    extra = lax.broadcasted_iota(jnp.int32, (LANES - HEAD_DIM, LANES), 0)

    def remote(source, target, sems, head, device):
        return pltpu.make_async_remote_copy(
            src_ref=source,
            dst_ref=target,
            send_sem=sems.at[0, head],
            recv_sem=sems.at[1, head],
            device_id=device,
            device_id_type=pl.DeviceIdType.MESH,
        )

    def core_copy(head):
        return remote(
            local_ref.at[(1 - core) * heads + head],
            core_recv.at[head],
            core_sems,
            head,
            {"space": 1 - core},
        )

    def pair_copy(head):
        return remote(pair_send.at[head], pair_recv.at[head], pair_sems, head, {"tm": pair})

    def chain_copy(head):
        return remote(chain_send.at[head], chain_recv.at[head], chain_sems, head, {"tm": ahead})

    def out_copy(head):
        mine = out_ref.at[core * heads + head]
        return remote(mine, mine, out_sems, head, {"space": 1 - core})

    barrier = pltpu.get_barrier_semaphore()

    def greet(device):
        pl.semaphore_signal(barrier, inc=1, device_id=device, device_id_type=pl.DeviceIdType.MESH)

    greet({"space": 1 - core})
    greet({"tm": pair})

    @pl.when(order < links - 1)
    def _():
        greet({"tm": ahead})

    @pl.when(order > 0)
    def _():
        greet({"tm": behind})

    peers = 2 + jnp.minimum(order, 1) + jnp.minimum(links - 1 - order, 1)
    pl.semaphore_wait(barrier, peers)

    def begin(head, _):
        core_copy(head).start()
        return 0

    lax.fori_loop(0, heads, begin, 0)

    def over_cores(head, _):
        core_copy(head).wait_recv()
        half = merge(
            local_ref[core * heads + head].astype(F32), core_recv[head].astype(F32), lane, extra
        )
        half_ref[head] = half
        pair_send[head] = half.astype(BF16)
        pair_copy(head).start()
        return 0

    lax.fori_loop(0, heads, over_cores, 0)

    def give(head, total):
        out_ref[core * heads + head] = total.astype(BF16)
        out_copy(head).start()

    def over_pairs(head, _):
        pair_copy(head).wait_recv()
        half = half_ref[head]
        both = merge(half, pair_recv[head].astype(F32), lane, extra)
        both_ref[head] = both

        @pl.when(order == 0)
        def _():
            @pl.when(order < links - 1)
            def _():
                chain_send[head] = both.astype(BF16)
                chain_copy(head).start()

            give(head, jnp.where(sums_both, both, half))

        return 0

    lax.fori_loop(0, heads, over_pairs, 0)

    @pl.when(order == links - 1)
    def _():
        work(*work_refs)

    @pl.when(order > 0)
    def _():
        def over_chain(head, _):
            both = both_ref[head]
            chain_copy(head).wait_recv()
            before = chain_recv[head].astype(F32)

            @pl.when(order < links - 1)
            def _():
                chain_send[head] = merge(before, both, lane, extra).astype(BF16)
                chain_copy(head).start()

            mine = jnp.where(sums_both, both, half_ref[head])
            give(head, merge(before, mine, lane, extra))
            return 0

        lax.fori_loop(0, heads, over_chain, 0)

    @pl.when(order < links - 1)
    def _():
        work(*work_refs)

    def finish(head, _):
        core_copy(head).wait_send()
        pair_copy(head).wait_send()

        @pl.when(order < links - 1)
        def _():
            chain_copy(head).wait_send()

        out_copy(head).wait()
        return 0

    lax.fori_loop(0, heads, finish, 0)


def forward_body(query_ref, grad_ref, local_ref, state_ref, attended_ref, query_grad_ref, out_ref):
    size = HEAD_DIM
    count = query_ref.shape[0]
    lane = lax.broadcasted_iota(jnp.int32, (size, LANES), 1)
    tail = lax.broadcasted_iota(jnp.int32, (count, LANES - size), 1)
    for head in range(HEADS):
        lanes = slice(head * size, (head + 1) * size)
        query_pre = query_ref[:, lanes]
        query = jnp.maximum(query_pre, 0)
        grad = grad_ref[:, lanes]
        cotangent = grad.astype(F32)
        state = state_ref[head]
        mixed = dot(query, state[:size], ((1,), (0,)))
        back = dot(grad, state[:, :size], ((1,), (1,)))
        centred = mixed[:, :size]
        mass = mixed[:, size : size + 1] + mixed[:, size + 1 : size + 2]
        inverse = 1.0 / (mass + 1.0)
        rows = state[size:].astype(F32)
        mean = rows[0:1, :size] + rows[1:2, :size]
        keys_row = rows[2:3, :size] + rows[3:4, :size]
        output = (centred + mass * mean) * inverse
        attended_ref[:, lanes] = (output + local_ref[:, lanes]).astype(BF16)
        along = back[:, size : size + 1] + back[:, size + 1 : size + 2]
        product = jnp.sum(cotangent * centred, axis=1, keepdims=True)
        grad_query = (back[:, :size] + ((along - product) * inverse) * keys_row) * inverse
        query_grad_ref[:, lanes] = jnp.where(
            query_pre.astype(F32) > 0, grad_query, 0.0
        ).astype(BF16)
        high, low = high_low(-(product + mass * along) * inverse)
        side = jnp.where(tail == 0, high, jnp.where(tail == 1, low, 0.0)).astype(BF16)
        scaled = (query.astype(F32) * inverse).astype(BF16)
        sums = dot(scaled, jnp.concatenate([grad, side], axis=1), ((0,), (0,)))
        total = sums[:, size : size + 1] + sums[:, size + 1 : size + 2]
        high, low = high_low(total)
        out_ref[head] = jnp.where(
            lane < size, sums, jnp.where(lane == size, high, jnp.where(lane == size + 1, low, 0.0))
        ).astype(BF16)


def backward_body(key_ref, value_ref, conv_ref, state_ref, key_grad_ref, value_grad_ref):
    size = HEAD_DIM
    count = key_ref.shape[0]
    ones = jnp.where(
        lax.broadcasted_iota(jnp.int32, (count, LANES - size), 1) < 2, 1.0, 0.0
    ).astype(BF16)
    for head in range(HEADS):
        lanes = slice(head * size, (head + 1) * size)
        key_pre = key_ref[:, lanes]
        state = state_ref[head]
        value = jnp.concatenate([value_ref[:, lanes], ones], axis=1)
        grad_key = dot(value, state, ((1,), (1,)))
        mixed = dot(jnp.maximum(key_pre, 0), state, ((1,), (0,)))
        key_grad_ref[:, lanes] = jnp.where(key_pre.astype(F32) > 0, grad_key, 0.0).astype(BF16)
        value_grad_ref[:, lanes] = (mixed[:, :size] + conv_ref[:, lanes]).astype(BF16)


def edge_rows(*blocks):
    place = lax.axis_index("space")
    last = blocks[0].shape[1] - 1
    own = jnp.stack(
        [lax.dynamic_index_in_dim(a[0], (1 - place) * last, 0, False) for a in blocks]
    )
    return lax.ppermute(own, "space", [(0, 1), (1, 0)])


def scan_over(local, merge, reverse, work=lambda: None, args=(), outs=()):
    half = (local.shape[0] // 2,) + local.shape[1:]
    sems = pltpu.SemaphoreType.DMA((2, half[0]))
    return pl.pallas_call(
        functools.partial(scan_body, merge, reverse, work, len(args)),
        out_shape=(struct(local.shape, BF16),) + tuple(outs),
        in_specs=[pl.BlockSpec(memory_space=pltpu.VMEM)] * (1 + len(args)),
        out_specs=(pl.BlockSpec(memory_space=pltpu.VMEM),) * (1 + len(outs)),
        scratch_shapes=[pltpu.VMEM(half, F32)] * 2 + [pltpu.VMEM(half, BF16)] * 5 + [sems] * 4,
        compiler_params=pltpu.CompilerParams(
            collective_id=int(reverse), has_side_effects=True, vmem_limit_bytes=VMEM_LIMIT
        ),
        cost_estimate=cost(25),
    )(local, *args)


def summed_over(x, axis):
    count = lax.axis_size(axis)
    if count & (count - 1):
        return lax.psum(x, axis)
    step = 1
    while step < count:
        x = x + lax.ppermute(x, axis, [(i, i ^ step) for i in range(count)])
        step *= 2
    return x


def shards(query_pre, key_pre, value_pre, grad_out, conv_taps):
    frames, rows, cols, width = value_pre.shape
    assert frames == 1 and width == HEADS * HEAD_DIM and lax.axis_size("space") == 2
    assert lax.axis_size("tm") % 2 == 0
    count = rows * cols
    flat = (count, width)
    query, key, value, grad = (
        a.reshape(flat) for a in (query_pre, key_pre, value_pre, grad_out)
    )
    partial = call(partial_body, struct((HEADS, LANES, LANES), BF16), key, value)
    edges = edge_rows(value_pre, grad_out)
    state, local, conv, taps_grad = scan_over(
        partial,
        merge_packed,
        False,
        lambda *refs: conv_body(rows, cols, *refs),
        (value, grad, edges, conv_taps.reshape(9, width)),
        (struct(flat, F32), struct(flat, F32), struct((9, width), F32)),
    )
    for axis in ("space", "tm"):
        taps_grad = summed_over(taps_grad, axis)
    taps_grad = taps_grad.reshape(3, 3, width)
    attended, query_grad, grad_partial = call(
        forward_body,
        (struct(flat, BF16), struct(flat, BF16), struct((HEADS, HEAD_DIM, LANES), BF16)),
        query,
        grad,
        local,
        state,
    )
    (grad_state,) = scan_over(grad_partial, add_packed, True)
    key_grad, value_grad = call(
        backward_body,
        (struct(flat, BF16), struct(flat, BF16)),
        key,
        value,
        conv,
        grad_state,
    )
    full = value_pre.shape
    return (
        attended.reshape(full),
        query_grad.reshape(full),
        key_grad.reshape(full),
        value_grad.reshape(full),
        taps_grad,
    )


def solution(mesh):
    tokens = P(("groups", "tm"), "space", None, None)
    return jax.shard_map(
        shards,
        mesh=mesh,
        in_specs=(tokens, tokens, tokens, tokens, P()),
        out_specs=(tokens, tokens, tokens, tokens, P("groups", None, None)),
        check_vma=False,
    )
```
